256 devices in a mesh: lat: 8 (over z), lon: 32 (over x, y, core).
Axes of the slice: x: 4, y: 4, z: 8, core: 2. Of those that a mesh axis runs over, the one named last changes fastest.
Arguments:
- inputs: bfloat16 [4, 128, 256, 1024], P(None, 'lat', 'lon'), may hold values from -6 to 6
- w_reduce: bfloat16 [1024, 256], replicated, may hold values from -0.1875 to 0.1875
- gain_reduce: float32 [256], replicated, may hold values from 0.1 to 1.9
- bias_reduce: float32 [256], replicated, may hold values from -3 to 3
- w_dilated: bfloat16 [3, 3, 256, 256], replicated, may hold values from -0.125 to 0.125
- gain_dilated: float32 [256], replicated, may hold values from 0.1 to 1.9
- bias_dilated: float32 [256], replicated, may hold values from -3 to 3
- w_expand: bfloat16 [256, 1024], replicated, may hold values from -0.375 to 0.375
- gain_expand: float32 [1024], replicated, may hold values from 0.1 to 1.9
- bias_expand: float32 [1024], replicated, may hold values from -3 to 3
- grad_out: bfloat16 [4, 128, 256, 1024], P(None, 'lat', 'lon'), may hold values from -6 to 6
- labels: int32 [4, 128, 256], P(None, 'lat', 'lon'), may hold values from 0 to 2
- class_weight: float32 [3], replicated, may hold values from 0.5 to 8
Outputs:
- grad_inputs: bfloat16 [4, 128, 256, 1024], P(None, 'lat', 'lon')
- grad_reduce: bfloat16 [1024, 256], replicated
- grad_dilated: bfloat16 [3, 3, 256, 256], replicated
- grad_expand: bfloat16 [256, 1024], replicated
The draws below stay inside these ranges and needn't reach their ends.
All inputs are finite; a program needn't handle non-finite values.
Results may differ from the reference program's by a relative error of at most 0.0079.
Values may be sent and summed in bfloat16 or wider, within the bound.
A program may use at most 64 MiB of HBM per device.

```python
import math
import jax
import jax.numpy as jnp
from jax import lax

C_IN = 1024
C_MID = 256
CLASSES = 3
BATCH = 4
HEIGHT = 128
WIDTH = 256


def touch_ends(drawn, stream_key, least, high):
    longest = drawn.shape.index(max(drawn.shape))
    spots = []
    for shift in (0, 1):
        where = [jax.random.randint(jax.random.fold_in(stream_key, axis), (), 0, length) for axis, length in enumerate(drawn.shape)]
        where[longest] = (where[longest] + shift) % drawn.shape[longest]
        spots.append(tuple(where))
    return drawn.at[spots[0]].set(least).at[spots[1]].set(high)


def block_levels(own_key, dims, split, least, high):
    gain, own = 1.0, jax.random.fold_in(own_key, 6)
    for dim, shards_of in split:
        heights = jnp.exp(jax.random.uniform(jax.random.fold_in(own, dim), (shards_of,), jnp.float32, least / len(split), high / len(split)))
        gain = gain * jnp.repeat(heights, dims[dim] // shards_of).reshape([-1 if axis == dim else 1 for axis in range(len(dims))])
    return gain


def centred(rng, extent, deviation, most, split=(), kind=jnp.bfloat16):
    result = jax.random.normal(rng, extent, jnp.float32) * deviation
    if len(split) > 0:
        result = block_levels(rng, extent, split, -0.22, 0.18) * result
    return jnp.clip(result, min=-most, max=most).astype(kind)


def setup_inputs(seed: int = 0) -> dict:
    streams_of = jax.random.split(jax.random.key(seed), 14)
    inputs = centred(streams_of[0], (BATCH, HEIGHT, WIDTH, C_IN), 1.0, 6.0, ((1, 8), (2, 32)))
    w_reduce = centred(streams_of[1], (C_IN, C_MID), C_IN ** -0.5, 0.1875)
    gain_reduce = jnp.clip(1.0 + 0.18 * jax.random.normal(streams_of[2], (C_MID,), jnp.float32), 0.1, 1.9)
    bias_reduce = centred(streams_of[3], (C_MID,), 0.5, 3.0, (), jnp.float32)
    w_dilated = centred(streams_of[4], (3, 3, C_MID, C_MID), (9 * C_MID) ** -0.5, 0.125)
    gain_dilated = jnp.clip(1.0 + 0.18 * jax.random.normal(streams_of[5], (C_MID,), jnp.float32), 0.1, 1.9)
    bias_dilated = centred(streams_of[6], (C_MID,), 0.5, 3.0, (), jnp.float32)
    w_expand = centred(streams_of[7], (C_MID, C_IN), C_MID ** -0.5, 0.375)
    gain_expand = jnp.clip(1.0 + 0.18 * jax.random.normal(streams_of[8], (C_IN,), jnp.float32), 0.1, 1.9)
    bias_expand = centred(streams_of[9], (C_IN,), 0.5, 3.0, (), jnp.float32)
    grad_out = centred(streams_of[10], (BATCH, HEIGHT, WIDTH, C_IN), 1.0, 6.0, ((1, 8), (2, 32)))
    labels = touch_ends(jax.random.randint(streams_of[11], (BATCH, HEIGHT, WIDTH), 0, 3), jax.random.fold_in(streams_of[11], 1), 0, 2).astype(jnp.int32)
    class_weight = jnp.clip(jnp.exp(jax.random.uniform(streams_of[12], (CLASSES,), jnp.float32, math.log(0.5), math.log(8.0))), 0.5, 8.0)
    return dict(inputs=inputs, w_reduce=w_reduce, gain_reduce=gain_reduce, bias_reduce=bias_reduce, w_dilated=w_dilated, gain_dilated=gain_dilated, bias_dilated=bias_dilated, w_expand=w_expand, gain_expand=gain_expand, bias_expand=bias_expand, grad_out=grad_out, labels=labels, class_weight=class_weight)


def smooth(pre):
    return pre * jax.nn.sigmoid(pre)


def slope(pre):
    sig = jax.nn.sigmoid(pre)
    return sig * (1.0 + pre * (1.0 - sig))


def extend(field):
    cyclic = jnp.pad(field, ((0, 0), (2, 2), (0, 0)), mode="wrap")
    return jnp.pad(cyclic, ((2, 2), (0, 0), (0, 0)))


def gather_taps(padded, height, width, flipped):
    pieces = []
    for row_tap in range(3):
        for col_tap in range(3):
            off_row = 4 - 2 * row_tap if flipped else 2 * row_tap
            off_col = 4 - 2 * col_tap if flipped else 2 * col_tap
            pieces.append(padded[off_row:off_row + height, off_col:off_col + width, :])
    stacked = jnp.concatenate(pieces, axis=-1)
    return stacked.reshape(height * width, stacked.shape[-1])


def reference(inputs, w_reduce, gain_reduce, bias_reduce, w_dilated, gain_dilated, bias_dilated, w_expand, gain_expand, bias_expand, grad_out, labels, class_weight):
    height, width = inputs.shape[1], inputs.shape[2]
    chan_in, chan_mid = w_reduce.shape
    pixels = height * width
    kernel = w_dilated.reshape(9 * chan_mid, chan_mid)
    kernel_back = jnp.transpose(w_dilated, (0, 1, 3, 2)).reshape(9 * chan_mid, chan_mid)
    classes = jnp.arange(class_weight.shape[0], dtype=jnp.int32)

    def sample(carry, pieces):
        image, upstream, label_map = pieces
        flat_in = image.reshape(pixels, chan_in)
        pre_one = jnp.dot(flat_in, w_reduce, preferred_element_type=jnp.float32) * gain_reduce + bias_reduce
        mid_one = smooth(pre_one).astype(jnp.bfloat16)
        padded_one = extend(mid_one.reshape(height, width, chan_mid))
        taps_one = gather_taps(padded_one, height, width, False)
        pre_two = jnp.dot(taps_one, kernel, preferred_element_type=jnp.float32) * gain_dilated + bias_dilated
        mid_two = smooth(pre_two).astype(jnp.bfloat16)
        pre_three = jnp.dot(mid_two, w_expand, preferred_element_type=jnp.float32) * gain_expand + bias_expand + flat_in.astype(jnp.float32)
        pixel_weight = jnp.sum(jnp.where(label_map.reshape(pixels, 1) == classes, class_weight, 0.0), axis=-1)
        grad_full = upstream.reshape(pixels, chan_in).astype(jnp.float32) * pixel_weight[:, None] * slope(pre_three)
        grad_three = (grad_full * gain_expand).astype(jnp.bfloat16)
        sum_expand = jnp.dot(mid_two.T, grad_three, preferred_element_type=jnp.float32)
        grad_two = (jnp.dot(grad_three, w_expand.T, preferred_element_type=jnp.float32) * slope(pre_two) * gain_dilated).astype(jnp.bfloat16)
        sum_dilated = jnp.dot(taps_one.T, grad_two, preferred_element_type=jnp.float32)
        padded_two = extend(grad_two.reshape(height, width, chan_mid))
        taps_two = gather_taps(padded_two, height, width, True)
        grad_one = (jnp.dot(taps_two, kernel_back, preferred_element_type=jnp.float32) * slope(pre_one) * gain_reduce).astype(jnp.bfloat16)
        sum_reduce = jnp.dot(flat_in.T, grad_one, preferred_element_type=jnp.float32)
        grad_in = (jnp.dot(grad_one, w_reduce.T, preferred_element_type=jnp.float32) + grad_full).astype(jnp.bfloat16)
        carry = (carry[0] + sum_reduce, carry[1] + sum_dilated, carry[2] + sum_expand)
        return carry, grad_in.reshape(height, width, chan_in)

    start = (jnp.zeros((chan_in, chan_mid), jnp.float32), jnp.zeros((9 * chan_mid, chan_mid), jnp.float32), jnp.zeros((chan_mid, chan_in), jnp.float32))
    totals, grad_inputs = lax.scan(sample, start, (inputs, grad_out, labels))
    grad_reduce = totals[0].astype(jnp.bfloat16)
    grad_dilated = totals[1].reshape(3, 3, chan_mid, chan_mid).astype(jnp.bfloat16)
    grad_expand = totals[2].astype(jnp.bfloat16)
    return (grad_inputs, grad_reduce, grad_dilated, grad_expand)
```

```python
import functools
import math

import jax
import jax.numpy as jnp
from jax import lax
from jax.experimental import pallas as pl
from jax.experimental.pallas import tpu as pltpu
from jax.sharding import PartitionSpec as P

MESH = pl.DeviceIdType.MESH
F32, BF16 = jnp.float32, jnp.bfloat16


def smooth(pre):
    return pre * jax.nn.sigmoid(pre)


def slope(pre):
    sig = jax.nn.sigmoid(pre)
    return sig * (1.0 + pre * (1.0 - sig))


def dot(left, right):
    return jnp.dot(left, right, preferred_element_type=F32)


def dot_rt(left, right):
    return lax.dot_general(left, right, (((1,), (1,)), ((), ())), preferred_element_type=F32)


def dot_lt(left, right):
    return lax.dot_general(left, right, (((0,), (0,)), ((), ())), preferred_element_type=F32)


def up(n, m):
    return -(-n // m) * m


class Term:
    def __init__(self, rows_a, rows_b, ring, depth):
        self.ra, self.rb, self.rows = rows_a, rows_b, rows_a + rows_b
        self.start = (0, rows_a)
        self.part = (rows_a, rows_b)
        self.first = (rows_a // ring, rows_b // ring)
        self.second = (rows_a // ring**2, rows_b // ring**2)
        self.joined = sum(self.second)
        self.zrows = up(self.joined, 8 * depth) // depth

    def scratch(self, ring, depth):
        return [
            pltpu.VMEM((2, self.rows, 128), BF16),
            pltpu.VMEM((self.rows, 128), BF16),
            pltpu.VMEM((self.rows, 128), BF16),
            pltpu.VMEM((ring - 1, self.first[0], 128), BF16),
            pltpu.VMEM((ring - 1, self.first[1], 128), BF16),
            pltpu.VMEM((self.first[0], 128), BF16),
            pltpu.VMEM((self.first[1], 128), BF16),
            pltpu.VMEM((ring - 1, self.second[0], 128), BF16),
            pltpu.VMEM((ring - 1, self.second[1], 128), BF16),
            pltpu.VMEM((depth * self.zrows, 128), F32),
            pltpu.VMEM((depth - 1, self.zrows, 128), F32),
            pltpu.VMEM((self.zrows, 128), F32),
            pltpu.VMEM((depth * self.zrows, 128), F32),
            pltpu.VMEM((2, self.rows, 128), BF16),
        ]


def kernel(ring, depth, terms, dims, *refs):
    batch, height, width, chan_in, chan_mid = dims
    pixels = batch * height * width
    h2n, w2n = height // 2, width // 2
    lon_n = ring * ring * 2
    (x_hbm, wr_hbm, wd_hbm, we_hbm, go_hbm, gr, br, gd, bd, ge, be, pw,
     gi_hbm, gred_hbm, gdil_hbm, gexp_hbm,
     x_v, wr_v, wd_v, we_v, go_v, perm, back, pre_one, slope_two, gfull, gthree, p_one, p_two, gi_v,
     *rest) = refs
    n_bufs = 14
    bufs = [rest[n_bufs * i : n_bufs * (i + 1)] for i in range(3)]
    load_sem, store_sem, send_sem, recv_sem = rest[3 * n_bufs :]

    lat, lon = lax.axis_index("lat"), lax.axis_index("lon")
    core, plane = lon % 2, lon // 2
    gx, gy = plane // ring, plane % ring

    loads = [
        pltpu.make_async_copy(src, dst, load_sem.at[i])
        for i, (src, dst) in enumerate(
            [(x_hbm, x_v), (wr_hbm, wr_v), (wd_hbm, wd_v), (we_hbm, we_v), (go_hbm, go_v)]
        )
    ]
    for load in loads:
        load.start()

    def at_xy(ax, ay):
        return (lat, (ax * ring + ay) * 2 + core)

    barrier = pltpu.get_barrier_semaphore()
    greet = [(lat, lon + 1 - 2 * core)]
    greet += [at_xy((gx + s) % ring, gy) for s in range(1, ring)]
    greet += [at_xy(gx, (gy + s) % ring) for s in range(1, ring)]
    greet += [((lat + s) % depth, lon) for s in range(1, depth)]
    for dl in (-1, 0, 1):
        for dw in (-1, 1):
            greet.append(((lat + dl + depth) % depth, (lon + dw + lon_n) % lon_n))
    for device in greet:
        pl.semaphore_signal(barrier, inc=1, device_id=device, device_id_type=MESH)

    def natural(p):
        return (
            ((p // 4) % batch) * (height * width)
            + (2 * (p // (16 * w2n)) + (p // 2) % 2) * width
            + 2 * ((p // 16) % w2n)
            + p % 2
        )

    lanes = lax.broadcasted_iota(jnp.int32, (pixels, 128), 1)
    rows = lax.broadcasted_iota(jnp.int32, (pixels, 128), 0)
    source = natural(lax.broadcasted_iota(jnp.int32, (pixels, 1), 0))
    for j in range(pixels // 128):
        cols = slice(j * 128, (j + 1) * 128)
        perm[:, cols] = jnp.where(source == lanes + j * 128, 1.0, 0.0).astype(BF16)
        target = natural(lax.broadcasted_iota(jnp.int32, (1, 128), 1) + j * 128)
        back[:, cols] = jnp.where(target == rows, 1.0, 0.0).astype(BF16)

    copies = []

    def remote(src, dst, device):
        i = len(copies)
        copy = pltpu.make_async_remote_copy(
            src_ref=src,
            dst_ref=dst,
            send_sem=send_sem.at[i],
            recv_sem=recv_sem.at[i],
            device_id=device,
            device_id_type=MESH,
        )
        copies.append(copy)
        return copy

    def send(src, dst, device):
        copy = remote(src, dst, device)
        copy.start()
        return copy

    guarded = []

    def halo(p_ref):
        hi, wi = slice(1, 1 + h2n), slice(1, 1 + w2n)

        @pl.when(lat == 0)
        def _():
            p_ref[0] = jnp.zeros_like(p_ref[0])

        @pl.when(lat == depth - 1)
        def _():
            p_ref[h2n + 1] = jnp.zeros_like(p_ref[h2n + 1])

        west, east = (lon + lon_n - 1) % lon_n, (lon + 1) % lon_n
        plan = []
        for dl in (0, -1, 1):
            row_src = {0: hi, -1: 1, 1: h2n}[dl]
            row_dst = {0: hi, -1: h2n + 1, 1: 0}[dl]
            there = (lat + dl + depth) % depth
            for dw in (0, -1, 1):
                if dl == 0 and dw == 0:
                    continue
                col_src = {0: wi, -1: 1, 1: w2n}[dw]
                col_dst = {0: wi, -1: w2n + 1, 1: 0}[dw]
                device = (there, {0: lon, -1: west, 1: east}[dw])
                copy = remote(p_ref.at[row_src, col_src], p_ref.at[row_dst, col_dst], device)
                plan.append((dl, copy))

        def sends(copy):
            return copy.start

        def on(dl, receiving, action):
            if dl == 0:
                action()
                return
            toward_low = (dl == -1) != receiving
            pl.when(lat > 0 if toward_low else lat < depth - 1)(action)

        for dl, copy in plan:
            on(dl, False, copy.start)
        guarded.extend((dl, copy, on) for dl, copy in plan)

        def wait():
            for dl, copy in plan:
                on(dl, True, copy.wait_recv)

        return wait

    def tap(p_ref, row, col):
        return p_ref[row : row + h2n, col : col + w2n].reshape(pixels, chan_mid)

    def to_natural(value):
        high = value.astype(BF16)
        low = (value - high.astype(F32)).astype(BF16)
        return dot(back[...], high) + dot(back[...], low)

    sibling = (lat, lon + 1 - 2 * core)

    def put_term(t, first_row, value):
        own = bufs[t][0]
        n = value.shape[0]
        own[0, first_row : first_row + n] = value[:, :128].astype(BF16)
        own[1, first_row : first_row + n] = value[:, 128:].astype(BF16)

    def core_send(t, part):
        term, b = terms[t], bufs[t]
        span = slice(term.start[part], term.start[part] + term.part[part])
        return send(b[0].at[1 - core, span], b[1].at[span], sibling)

    def ring_pos(part, step):
        return (gx, gy)[part ^ step]

    def ring_dev(part, step, s):
        if part ^ step == 0:
            return at_xy((gx + s) % ring, gy)
        return at_xy(gx, (gy + s) % ring)

    def pair_and_first(t, part, arrived):
        term, b = terms[t], bufs[t]
        arrived.wait_recv()
        lo, n = term.start[part], term.part[part]
        span = slice(lo, lo + n)
        b[2][span] = (b[0][core, span].astype(F32) + b[1][span].astype(F32)).astype(BF16)
        step = term.first[part]
        out = []
        for s in range(1, ring):
            peer = (ring_pos(part, 0) + s) % ring
            src = b[2].at[pl.ds(pl.multiple_of(lo + peer * step, 16), step)]
            out.append(send(src, b[3 + part].at[s - 1], ring_dev(part, 0, s)))
        return out

    def second(t, part, arrived):
        term, b = terms[t], bufs[t]
        for copy in arrived:
            copy.wait_recv()
        lo, n = term.start[part], term.first[part]
        mine = pl.ds(pl.multiple_of(lo + ring_pos(part, 0) * n, 16), n)
        total = b[2][mine].astype(F32)
        for s in range(ring - 1):
            total = total + b[3 + part][s].astype(F32)
        b[5 + part][...] = total.astype(BF16)
        step = term.second[part]
        out = []
        for s in range(1, ring):
            peer = (ring_pos(part, 1) + s) % ring
            src = b[5 + part].at[pl.ds(pl.multiple_of(peer * step, 16), step)]
            out.append(send(src, b[7 + part].at[s - 1], ring_dev(part, 1, s)))
        return out

    def third(t, arrived):
        term, b = terms[t], bufs[t]
        at = 0
        for part in (0, 1):
            for copy in arrived[part]:
                copy.wait_recv()
            n = term.second[part]
            mine = pl.ds(pl.multiple_of(ring_pos(part, 1) * n, 16), n)
            total = b[5 + part][mine].astype(F32)
            for s in range(ring - 1):
                total = total + b[7 + part][s].astype(F32)
            b[9][at : at + n] = total
            at += n
        if at < depth * term.zrows:
            b[9][at:] = jnp.zeros((depth * term.zrows - at, 128), F32)
        out = []
        for s in range(1, depth):
            peer = (lat + s) % depth
            src = b[9].at[pl.ds(pl.multiple_of(peer * term.zrows, 8), term.zrows)]
            out.append(send(src, b[10].at[s - 1], (peer, lon)))
        return out

    def fourth(t, arrived):
        term, b = terms[t], bufs[t]
        for copy in arrived:
            copy.wait_recv()
        mine = pl.ds(pl.multiple_of(lat * term.zrows, 8), term.zrows)
        total = b[9][mine]
        for s in range(depth - 1):
            total = total + b[10][s]
        b[11][...] = total
        b[12][mine] = total
        return [
            send(b[11], b[12].at[mine], ((lat + s) % depth, lon)) for s in range(1, depth)
        ]

    def fifth(t, arrived):
        term, b = terms[t], bufs[t]
        for copy in arrived:
            copy.wait_recv()
        at, outs = 0, []
        for part in (0, 1):
            n = term.second[part]
            place = term.start[part] + ring_pos(part, 0) * term.first[part] + ring_pos(part, 1) * n
            here = pl.ds(pl.multiple_of(place, 16), n)
            b[13][core, here] = b[12][at : at + n].astype(BF16)
            at += n
            block = b[13].at[core, here]
            outs.append([send(block, block, ring_dev(part, 1, s)) for s in range(1, ring)])
        return outs

    def sixth(t, arrived):
        term, b = terms[t], bufs[t]
        outs = []
        for part in (0, 1):
            for copy in arrived[part]:
                copy.wait_recv()
            n = term.first[part]
            place = term.start[part] + ring_pos(part, 0) * n
            block = b[13].at[core, pl.ds(pl.multiple_of(place, 16), n)]
            outs.append([send(block, block, ring_dev(part, 0, s)) for s in range(1, ring)])
        return outs

    def seventh(t, arrived):
        b = bufs[t]
        for part in (0, 1):
            for copy in arrived[part]:
                copy.wait_recv()
        return send(b[13].at[core], b[13].at[core], sibling)

    stores = []

    def store(src, dst):
        copy = pltpu.make_async_copy(src, dst, store_sem.at[len(stores)])
        copy.start()
        stores.append(copy)

    loads[0].wait()
    loads[1].wait()
    pre_one[...] = dot(x_v[...], wr_v[...]) * gr[...] + br[...]
    mid_one = smooth(pre_one[...]).astype(BF16)
    hi, wi = slice(1, 1 + h2n), slice(1, 1 + w2n)
    p_one[hi, wi] = dot(perm[...], mid_one).astype(BF16).reshape(h2n, w2n, 16, chan_mid)
    pl.semaphore_wait(barrier, len(greet))
    wait_one = halo(p_one)
    for load in loads[2:]:
        load.wait()
    total = dot(tap(p_one, 1, 1), wd_v[4])
    wait_one()
    for i in (0, 1, 2, 3, 5, 6, 7, 8):
        total = total + dot(tap(p_one, i // 3, i % 3), wd_v[i])
    pre_two = to_natural(total * gd[...] + bd[...])
    mid_two = smooth(pre_two).astype(BF16)
    slope_two[...] = slope(pre_two) * gd[...]

    blocks = chan_in // 256
    total = None
    for j in range(blocks):
        cols = slice(j * 256, (j + 1) * 256)
        w_block = we_v[:, cols]
        pre_three = dot(mid_two, w_block) * ge[:, cols] + be[:, cols] + x_v[:, cols].astype(F32)
        full = go_v[:, cols].astype(F32) * pw[...] * slope(pre_three)
        gfull[:, cols] = full
        grad_three = (full * ge[:, cols]).astype(BF16)
        gthree[:, cols] = grad_three
        term = dot_rt(grad_three, w_block)
        total = term if total is None else total + term
    grad_two = (total * slope_two[...]).astype(BF16)
    p_two[hi, wi] = dot(perm[...], grad_two).astype(BF16).reshape(h2n, w2n, 16, chan_mid)
    wait_two = halo(p_two)

    for j in range(blocks):
        put_term(0, j * 256, dot_lt(mid_two, gthree[:, j * 256 : (j + 1) * 256]))
    e_core = [core_send(0, 0), core_send(0, 1)]
    center = tap(p_two, 1, 1)
    taps_a = terms[1].ra // chan_mid
    d_core = []
    for i in range(9):
        put_term(1, i * chan_mid, dot_lt(tap(p_one, i // 3, i % 3), center))
        if i == taps_a - 1:
            d_core.append(core_send(1, 0))
    d_core.append(core_send(1, 1))
    e_first = [pair_and_first(0, part, e_core[part]) for part in (0, 1)]

    total = dot_rt(center, wd_v[4])
    wait_two()
    for i in (0, 1, 2, 3, 5, 6, 7, 8):
        total = total + dot_rt(tap(p_two, 2 - i // 3, 2 - i % 3), wd_v[i])
    grad_one = (to_natural(total) * slope(pre_one[...]) * gr[...]).astype(BF16)
    r_core = []
    for j in range(2):
        half = chan_in // 2
        put_term(2, j * half, dot_lt(x_v[:, j * half : (j + 1) * half], grad_one))
        r_core.append(core_send(2, j))
    d_first = [pair_and_first(1, part, d_core[part]) for part in (0, 1)]
    e_second = [second(0, part, e_first[part]) for part in (0, 1)]
    for j in range(blocks):
        cols = slice(j * 256, (j + 1) * 256)
        gi_v[:, cols] = (dot_rt(grad_one, wr_v[cols, :]) + gfull[:, cols]).astype(BF16)
    store(gi_v, gi_hbm)
    r_first = [pair_and_first(2, part, r_core[part]) for part in (0, 1)]
    e_third = third(0, e_second)
    d_second = [second(1, part, d_first[part]) for part in (0, 1)]
    r_second = [second(2, part, r_first[part]) for part in (0, 1)]
    d_third = third(1, d_second)
    e_fourth = fourth(0, e_third)
    r_third = third(2, r_second)
    d_fourth = fourth(1, d_third)
    e_fifth = fifth(0, e_fourth)
    r_fourth = fourth(2, r_third)
    d_fifth = fifth(1, d_fourth)
    e_sixth = sixth(0, e_fifth)
    r_fifth = fifth(2, r_fourth)
    d_sixth = sixth(1, d_fifth)
    e_last = seventh(0, e_sixth)
    r_sixth = sixth(2, r_fifth)
    d_last = seventh(1, d_sixth)
    r_last = seventh(2, r_sixth)

    e_last.wait_recv()
    for side in (0, 1):
        for j in range(blocks):
            first = j * 256 + side * 128
            store(
                bufs[0][13].at[side, j * 256 : (j + 1) * 256], gexp_hbm.at[:, first : first + 128]
            )
    d_last.wait_recv()
    for side in (0, 1):
        store(bufs[1][13].at[side], gdil_hbm.at[:, side * 128 : (side + 1) * 128])
    r_last.wait_recv()
    for side in (0, 1):
        store(bufs[2][13].at[side], gred_hbm.at[:, side * 128 : (side + 1) * 128])
    halo_copies = {id(copy) for _, copy, _ in guarded}
    for dl, copy, on in guarded:
        on(dl, False, copy.wait_send)
    for copy in copies:
        if id(copy) not in halo_copies:
            copy.wait_send()
    for copy in stores:
        copy.wait()


def per_device(
    ring,
    depth,
    inputs,
    w_reduce,
    gain_reduce,
    bias_reduce,
    w_dilated,
    gain_dilated,
    bias_dilated,
    w_expand,
    gain_expand,
    bias_expand,
    grad_out,
    labels,
    class_weight,
):
    batch, height, width, chan_in = inputs.shape
    chan_mid = w_reduce.shape[1]
    pixels = batch * height * width
    classes = jnp.arange(class_weight.shape[0], dtype=jnp.int32)
    weight = jnp.sum(
        jnp.where(labels.reshape(pixels, 1) == classes, class_weight, 0.0), axis=-1, keepdims=True
    )
    half = chan_in // 2
    terms = [
        Term(half, half, ring, depth),
        Term(5 * chan_mid, 4 * chan_mid, ring, depth),
        Term(half, half, ring, depth),
    ]
    scratch = [
        pltpu.VMEM((pixels, chan_in), BF16),
        pltpu.VMEM((chan_in, chan_mid), BF16),
        pltpu.VMEM((9, chan_mid, chan_mid), BF16),
        pltpu.VMEM((chan_mid, chan_in), BF16),
        pltpu.VMEM((pixels, chan_in), BF16),
        pltpu.VMEM((pixels, pixels), BF16),
        pltpu.VMEM((pixels, pixels), BF16),
        pltpu.VMEM((pixels, chan_mid), F32),
        pltpu.VMEM((pixels, chan_mid), F32),
        pltpu.VMEM((pixels, chan_in), F32),
        pltpu.VMEM((pixels, chan_in), BF16),
        pltpu.VMEM((height // 2 + 2, width // 2 + 2, 16, chan_mid), BF16),
        pltpu.VMEM((height // 2 + 2, width // 2 + 2, 16, chan_mid), BF16),
        pltpu.VMEM((pixels, chan_in), BF16),
    ]
    for term in terms:
        scratch += term.scratch(ring, depth)
    per_term = 2 + 12 * (ring - 1) // 3 * 2 + 2 * (depth - 1) + 1
    n_remote = 16 + 3 * (2 + 8 * (ring - 1) + 2 * (depth - 1) + 1)
    scratch += [
        pltpu.SemaphoreType.DMA((5,)),
        pltpu.SemaphoreType.DMA((2 * (chan_in // 256) + 5,)),
        pltpu.SemaphoreType.DMA((n_remote,)),
        pltpu.SemaphoreType.DMA((n_remote,)),
    ]
    anywhere = pl.BlockSpec(memory_space=pl.ANY)
    vmem = pl.BlockSpec(memory_space=pltpu.VMEM)
    grad_inputs, grad_reduce, grad_dilated, grad_expand = pl.pallas_call(
        functools.partial(
            kernel, ring, depth, terms, (batch, height, width, chan_in, chan_mid)
        ),
        out_shape=(
            jax.ShapeDtypeStruct((pixels, chan_in), BF16),
            jax.ShapeDtypeStruct((chan_in, chan_mid), BF16),
            jax.ShapeDtypeStruct((9 * chan_mid, chan_mid), BF16),
            jax.ShapeDtypeStruct((chan_mid, chan_in), BF16),
        ),
        in_specs=[anywhere] * 5 + [vmem] * 7,
        out_specs=(anywhere,) * 4,
        scratch_shapes=scratch,
        compiler_params=pltpu.CompilerParams(
            collective_id=0, has_side_effects=True, vmem_limit_bytes=60 * 2**20
        ),
    )(
        inputs.reshape(pixels, chan_in),
        w_reduce,
        w_dilated.reshape(9, chan_mid, chan_mid),
        w_expand,
        grad_out.reshape(pixels, chan_in),
        gain_reduce.reshape(1, -1),
        bias_reduce.reshape(1, -1),
        gain_dilated.reshape(1, -1),
        bias_dilated.reshape(1, -1),
        gain_expand.reshape(1, -1),
        bias_expand.reshape(1, -1),
        weight,
    )
    return (
        grad_inputs.reshape(batch, height, width, chan_in),
        grad_reduce,
        grad_dilated.reshape(3, 3, chan_mid, chan_mid),
        grad_expand,
    )


def solution(mesh):
    ring = math.isqrt(mesh.shape["lon"] // 2)
    field = P(None, "lat", "lon", None)
    return jax.shard_map(
        functools.partial(per_device, ring, mesh.shape["lat"]),
        mesh=mesh,
        in_specs=(field,) + (P(),) * 9 + (field, P(None, "lat", "lon"), P()),
        out_specs=(field, P(), P(), P()),
        check_vma=False,
    )
```

```python
import functools
import math

import jax
import jax.numpy as jnp
from jax import lax
from jax.experimental import pallas as pl
from jax.experimental.pallas import tpu as pltpu
from jax.sharding import PartitionSpec as P

MESH = pl.DeviceIdType.MESH
F32, BF16 = jnp.float32, jnp.bfloat16


def smooth(pre):
    return pre * jax.nn.sigmoid(pre)


def slope(pre):
    sig = jax.nn.sigmoid(pre)
    return sig * (1.0 + pre * (1.0 - sig))


def dot(left, right):
    return jnp.dot(left, right, preferred_element_type=F32)


def dot_rt(left, right):
    return lax.dot_general(left, right, (((1,), (1,)), ((), ())), preferred_element_type=F32)


def dot_lt(left, right):
    return lax.dot_general(left, right, (((0,), (0,)), ((), ())), preferred_element_type=F32)


def up(n, m):
    return -(-n // m) * m


class Term:
    def __init__(self, rows_a, rows_b, ring, depth):
        self.ra, self.rb, self.rows = rows_a, rows_b, rows_a + rows_b
        self.start = (0, rows_a)
        self.part = (rows_a, rows_b)
        self.first = (rows_a // ring, rows_b // ring)
        self.second = (rows_a // ring**2, rows_b // ring**2)
        self.joined = sum(self.second)
        self.zrows = up(self.joined, 8 * depth) // depth

    def scratch(self, ring, depth):
        return [
            pltpu.VMEM((2, self.rows, 128), BF16),
            pltpu.VMEM((self.rows, 128), BF16),
            pltpu.VMEM((self.rows, 128), BF16),
            pltpu.VMEM((ring - 1, self.first[0], 128), BF16),
            pltpu.VMEM((ring - 1, self.first[1], 128), BF16),
            pltpu.VMEM((self.first[0], 128), BF16),
            pltpu.VMEM((self.first[1], 128), BF16),
            pltpu.VMEM((ring - 1, self.second[0], 128), BF16),
            pltpu.VMEM((ring - 1, self.second[1], 128), BF16),
            pltpu.VMEM((depth * self.zrows, 128), F32),
            pltpu.VMEM((depth - 1, self.zrows, 128), BF16),
            pltpu.VMEM((self.zrows, 128), BF16),
            pltpu.VMEM((depth, self.zrows, 128), BF16),
            pltpu.VMEM((2, self.rows, 128), BF16),
            pltpu.VMEM((depth, self.zrows, 128), BF16),
        ]


def kernel(ring, depth, terms, dims, *refs):
    batch, height, width, chan_in, chan_mid = dims
    pixels = batch * height * width
    h2n, w2n = height // 2, width // 2
    lon_n = ring * ring * 2
    (x_hbm, wr_hbm, gr_hbm, br_hbm, wd_hbm, gd_hbm, bd_hbm, we_hbm, ge_hbm, be_hbm, go_hbm,
     label_hbm, class_weight,
     gi_hbm, gred_hbm, gdil_hbm, gexp_hbm,
     x_v, wr_v, gr, br, wd_v, gd, bd, we_v, ge, be, go_v, label_v,
     pw, perm, back, pre_one, slope_two, gfull, gthree, p_one, p_two, gi_v,
     *rest) = refs
    n_bufs = 15
    bufs = [rest[n_bufs * i : n_bufs * (i + 1)] for i in range(3)]
    load_sem, store_sem, send_sem, recv_sem = rest[3 * n_bufs :]

    lat, lon = lax.axis_index("lat"), lax.axis_index("lon")
    core, plane = lon % 2, lon // 2
    gx, gy = plane // ring, plane % ring

    loads = [
        pltpu.make_async_copy(src, dst, load_sem.at[i])
        for i, (src, dst) in enumerate(
            [
                (x_hbm, x_v), (wr_hbm, wr_v), (gr_hbm, gr), (br_hbm, br),
                (label_hbm, label_v), (wd_hbm, wd_v), (gd_hbm, gd), (bd_hbm, bd),
                (we_hbm, we_v), (ge_hbm, ge), (be_hbm, be), (go_hbm, go_v),
            ]
        )
    ]
    for load in loads:
        load.start()

    def at_xy(ax, ay):
        return (lat, (ax * ring + ay) * 2 + core)

    barrier = pltpu.get_barrier_semaphore()
    greet = [(lat, lon + 1 - 2 * core)]
    greet += [at_xy((gx + s) % ring, gy) for s in range(1, ring)]
    greet += [at_xy(gx, (gy + s) % ring) for s in range(1, ring)]
    greet += [((lat + s) % depth, lon) for s in range(1, depth)]
    for dl in (-1, 0, 1):
        for dw in (-1, 1):
            greet.append(((lat + dl + depth) % depth, (lon + dw + lon_n) % lon_n))
    for device in greet:
        pl.semaphore_signal(barrier, inc=1, device_id=device, device_id_type=MESH)

    def natural(p):
        return (
            ((p // 4) % batch) * (height * width)
            + (2 * (p // (16 * w2n)) + (p // 2) % 2) * width
            + 2 * ((p // 16) % w2n)
            + p % 2
        )

    lanes = lax.broadcasted_iota(jnp.int32, (pixels, 128), 1)
    rows = lax.broadcasted_iota(jnp.int32, (pixels, 128), 0)
    source = natural(lax.broadcasted_iota(jnp.int32, (pixels, 1), 0))
    for j in range(pixels // 128):
        cols = slice(j * 128, (j + 1) * 128)
        perm[:, cols] = jnp.where(source == lanes + j * 128, 1.0, 0.0).astype(BF16)
        target = natural(lax.broadcasted_iota(jnp.int32, (1, 128), 1) + j * 128)
        back[:, cols] = jnp.where(target == rows, 1.0, 0.0).astype(BF16)

    copies = []

    def remote(src, dst, device):
        i = len(copies)
        copy = pltpu.make_async_remote_copy(
            src_ref=src,
            dst_ref=dst,
            send_sem=send_sem.at[i],
            recv_sem=recv_sem.at[i],
            device_id=device,
            device_id_type=MESH,
        )
        copies.append(copy)
        return copy

    def send(src, dst, device):
        copy = remote(src, dst, device)
        copy.start()
        return copy

    guarded = []

    def halo(p_ref):
        hi, wi = slice(1, 1 + h2n), slice(1, 1 + w2n)

        @pl.when(lat == 0)
        def _():
            p_ref[0] = jnp.zeros_like(p_ref[0])

        @pl.when(lat == depth - 1)
        def _():
            p_ref[h2n + 1] = jnp.zeros_like(p_ref[h2n + 1])

        west, east = (lon + lon_n - 1) % lon_n, (lon + 1) % lon_n
        plan = []
        for dl in (0, -1, 1):
            row_src = {0: hi, -1: 1, 1: h2n}[dl]
            row_dst = {0: hi, -1: h2n + 1, 1: 0}[dl]
            there = (lat + dl + depth) % depth
            for dw in (0, -1, 1):
                if dl == 0 and dw == 0:
                    continue
                col_src = {0: wi, -1: 1, 1: w2n}[dw]
                col_dst = {0: wi, -1: w2n + 1, 1: 0}[dw]
                device = (there, {0: lon, -1: west, 1: east}[dw])
                copy = remote(p_ref.at[row_src, col_src], p_ref.at[row_dst, col_dst], device)
                plan.append((dl, copy))

        def sends(copy):
            return copy.start

        def on(dl, receiving, action):
            if dl == 0:
                action()
                return
            toward_low = (dl == -1) != receiving
            pl.when(lat > 0 if toward_low else lat < depth - 1)(action)

        for dl, copy in plan:
            on(dl, False, copy.start)
        guarded.extend((dl, copy, on) for dl, copy in plan)

        def wait():
            for dl, copy in plan:
                on(dl, True, copy.wait_recv)

        return wait

    def tap(p_ref, row, col):
        return p_ref[row : row + h2n, col : col + w2n].reshape(pixels, chan_mid)

    def to_natural(value):
        high = value.astype(BF16)
        low = (value - high.astype(F32)).astype(BF16)
        return dot(back[...], high) + dot(back[...], low)

    sibling = (lat, lon + 1 - 2 * core)

    def put_term(t, first_row, value):
        own = bufs[t][0]
        n = value.shape[0]
        own[0, first_row : first_row + n] = value[:, :128].astype(BF16)
        own[1, first_row : first_row + n] = value[:, 128:].astype(BF16)

    def core_send(t, part):
        term, b = terms[t], bufs[t]
        span = slice(term.start[part], term.start[part] + term.part[part])
        return send(b[0].at[1 - core, span], b[1].at[span], sibling)

    def ring_pos(part, step):
        return (gx, gy)[part ^ step]

    def ring_dev(part, step, s):
        if part ^ step == 0:
            return at_xy((gx + s) % ring, gy)
        return at_xy(gx, (gy + s) % ring)

    def pair_and_first(t, part, arrived):
        term, b = terms[t], bufs[t]
        arrived.wait_recv()
        lo, n = term.start[part], term.part[part]
        span = slice(lo, lo + n)
        b[2][span] = (b[0][core, span].astype(F32) + b[1][span].astype(F32)).astype(BF16)
        step = term.first[part]
        out = []
        for s in range(1, ring):
            peer = (ring_pos(part, 0) + s) % ring
            src = b[2].at[pl.ds(pl.multiple_of(lo + peer * step, 16), step)]
            out.append(send(src, b[3 + part].at[s - 1], ring_dev(part, 0, s)))
        return out

    def second(t, part, arrived):
        term, b = terms[t], bufs[t]
        for copy in arrived:
            copy.wait_recv()
        lo, n = term.start[part], term.first[part]
        mine = pl.ds(pl.multiple_of(lo + ring_pos(part, 0) * n, 16), n)
        total = b[2][mine].astype(F32)
        for s in range(ring - 1):
            total = total + b[3 + part][s].astype(F32)
        b[5 + part][...] = total.astype(BF16)
        step = term.second[part]
        out = []
        for s in range(1, ring):
            peer = (ring_pos(part, 1) + s) % ring
            src = b[5 + part].at[pl.ds(pl.multiple_of(peer * step, 16), step)]
            out.append(send(src, b[7 + part].at[s - 1], ring_dev(part, 1, s)))
        return out

    def third(t, arrived):
        term, b = terms[t], bufs[t]
        at = 0
        for part in (0, 1):
            for copy in arrived[part]:
                copy.wait_recv()
            n = term.second[part]
            mine = pl.ds(pl.multiple_of(ring_pos(part, 1) * n, 16), n)
            total = b[5 + part][mine].astype(F32)
            for s in range(ring - 1):
                total = total + b[7 + part][s].astype(F32)
            b[9][at : at + n] = total
            at += n
        if at < depth * term.zrows:
            b[9][at:] = jnp.zeros((depth * term.zrows - at, 128), F32)
        b[14][...] = b[9][...].reshape(depth, term.zrows, 128).astype(BF16)
        out = []
        for s in range(1, depth):
            peer = (lat + s) % depth
            out.append(send(b[14].at[peer], b[10].at[s - 1], (peer, lon)))
        return out

    def fourth(t, arrived):
        term, b = terms[t], bufs[t]
        for copy in arrived:
            copy.wait_recv()
        mine = pl.ds(pl.multiple_of(lat * term.zrows, 8), term.zrows)
        total = b[9][mine]
        for s in range(depth - 1):
            total = total + b[10][s].astype(F32)
        b[11][...] = total.astype(BF16)
        b[12][lat] = total.astype(BF16)
        return [
            send(b[11], b[12].at[lat], ((lat + s) % depth, lon)) for s in range(1, depth)
        ]

    def fifth(t, arrived):
        term, b = terms[t], bufs[t]
        for copy in arrived:
            copy.wait_recv()
        at, outs = 0, []
        whole = b[12][...].astype(F32).reshape(depth * term.zrows, 128)
        for part in (0, 1):
            n = term.second[part]
            place = term.start[part] + ring_pos(part, 0) * term.first[part] + ring_pos(part, 1) * n
            here = pl.ds(pl.multiple_of(place, 16), n)
            b[13][core, here] = whole[at : at + n].astype(BF16)
            at += n
            block = b[13].at[core, here]
            outs.append([send(block, block, ring_dev(part, 1, s)) for s in range(1, ring)])
        return outs

    def sixth(t, arrived):
        term, b = terms[t], bufs[t]
        outs = []
        for part in (0, 1):
            for copy in arrived[part]:
                copy.wait_recv()
            n = term.first[part]
            place = term.start[part] + ring_pos(part, 0) * n
            block = b[13].at[core, pl.ds(pl.multiple_of(place, 16), n)]
            outs.append([send(block, block, ring_dev(part, 0, s)) for s in range(1, ring)])
        return outs

    def seventh(t, arrived):
        b = bufs[t]
        for part in (0, 1):
            for copy in arrived[part]:
                copy.wait_recv()
        return send(b[13].at[core], b[13].at[core], sibling)

    stores = []

    def store(src, dst):
        copy = pltpu.make_async_copy(src, dst, store_sem.at[len(stores)])
        copy.start()
        stores.append(copy)

    for load in loads[:4]:
        load.wait()
    pre_one[...] = dot(x_v[...], wr_v[...]) * gr[...] + br[...]
    mid_one = smooth(pre_one[...]).astype(BF16)
    hi, wi = slice(1, 1 + h2n), slice(1, 1 + w2n)
    p_one[hi, wi] = dot(perm[...], mid_one).astype(BF16).reshape(h2n, w2n, 16, chan_mid)
    pl.semaphore_wait(barrier, len(greet))
    wait_one = halo(p_one)
    for load in loads[4:]:
        load.wait()
    lab_rows = batch * width
    pixel = lax.broadcasted_iota(jnp.int32, (pixels, lab_rows), 0)
    row = (pixel // (height * width)) * width + pixel % width
    row_hot = jnp.where(
        row == lax.broadcasted_iota(jnp.int32, (pixels, lab_rows), 1), 1.0, 0.0
    ).astype(BF16)
    picked = dot(row_hot, label_v[...].astype(F32).astype(BF16))
    pixel = lax.broadcasted_iota(jnp.int32, (pixels, height), 0)
    lane_hot = (pixel // width) % height == lax.broadcasted_iota(jnp.int32, (pixels, height), 1)
    label = jnp.sum(jnp.where(lane_hot, picked, 0.0), axis=1, keepdims=True)
    weight = class_weight[0, 0]
    for k in range(1, class_weight.shape[1]):
        weight = jnp.where(label > k - 0.5, class_weight[0, k], weight)
    pw[...] = jnp.broadcast_to(weight, pw.shape)
    total = dot(tap(p_one, 1, 1), wd_v[4])
    wait_one()
    for i in (0, 1, 2, 3, 5, 6, 7, 8):
        total = total + dot(tap(p_one, i // 3, i % 3), wd_v[i])
    pre_two = to_natural(total * gd[...] + bd[...])
    mid_two = smooth(pre_two).astype(BF16)
    slope_two[...] = slope(pre_two) * gd[...]

    blocks = chan_in // 256
    total = None
    for j in range(blocks):
        cols = slice(j * 256, (j + 1) * 256)
        w_block = we_v[:, cols]
        pre_three = dot(mid_two, w_block) * ge[:, cols] + be[:, cols] + x_v[:, cols].astype(F32)
        full = go_v[:, cols].astype(F32) * pw[...] * slope(pre_three)
        gfull[:, cols] = full
        grad_three = (full * ge[:, cols]).astype(BF16)
        gthree[:, cols] = grad_three
        term = dot_rt(grad_three, w_block)
        total = term if total is None else total + term
    grad_two = (total * slope_two[...]).astype(BF16)
    p_two[hi, wi] = dot(perm[...], grad_two).astype(BF16).reshape(h2n, w2n, 16, chan_mid)
    wait_two = halo(p_two)

    for j in range(blocks):
        put_term(0, j * 256, dot_lt(mid_two, gthree[:, j * 256 : (j + 1) * 256]))
    e_core = [core_send(0, 0), core_send(0, 1)]
    center = tap(p_two, 1, 1)
    taps_a = terms[1].ra // chan_mid
    d_core = []
    for i in range(9):
        put_term(1, i * chan_mid, dot_lt(tap(p_one, i // 3, i % 3), center))
        if i == taps_a - 1:
            d_core.append(core_send(1, 0))
            e_first = [pair_and_first(0, part, e_core[part]) for part in (0, 1)]
    d_core.append(core_send(1, 1))

    total = dot_rt(center, wd_v[4])
    wait_two()
    for i in (0, 1, 2, 3, 5, 6, 7, 8):
        total = total + dot_rt(tap(p_two, 2 - i // 3, 2 - i % 3), wd_v[i])
    grad_one = (to_natural(total) * slope(pre_one[...]) * gr[...]).astype(BF16)
    r_core = []
    for j in range(2):
        half = chan_in // 2
        put_term(2, j * half, dot_lt(x_v[:, j * half : (j + 1) * half], grad_one))
        r_core.append(core_send(2, j))
    d_first = [pair_and_first(1, part, d_core[part]) for part in (0, 1)]
    e_second = [second(0, part, e_first[part]) for part in (0, 1)]
    for j in range(blocks):
        cols = slice(j * 256, (j + 1) * 256)
        gi_v[:, cols] = (dot_rt(grad_one, wr_v[cols, :]) + gfull[:, cols]).astype(BF16)
    store(gi_v, gi_hbm)
    r_first = [pair_and_first(2, part, r_core[part]) for part in (0, 1)]
    e_third = third(0, e_second)
    d_second = [second(1, part, d_first[part]) for part in (0, 1)]
    r_second = [second(2, part, r_first[part]) for part in (0, 1)]
    d_third = third(1, d_second)
    e_fourth = fourth(0, e_third)
    r_third = third(2, r_second)
    d_fourth = fourth(1, d_third)
    e_fifth = fifth(0, e_fourth)
    r_fourth = fourth(2, r_third)
    d_fifth = fifth(1, d_fourth)
    e_sixth = sixth(0, e_fifth)
    r_fifth = fifth(2, r_fourth)
    d_sixth = sixth(1, d_fifth)
    e_last = seventh(0, e_sixth)
    r_sixth = sixth(2, r_fifth)
    d_last = seventh(1, d_sixth)
    r_last = seventh(2, r_sixth)

    e_last.wait_recv()
    for side in (0, 1):
        for j in range(blocks):
            first = j * 256 + side * 128
            store(
                bufs[0][13].at[side, j * 256 : (j + 1) * 256], gexp_hbm.at[:, first : first + 128]
            )
    d_last.wait_recv()
    for side in (0, 1):
        store(bufs[1][13].at[side], gdil_hbm.at[:, side * 128 : (side + 1) * 128])
    r_last.wait_recv()
    for side in (0, 1):
        store(bufs[2][13].at[side], gred_hbm.at[:, side * 128 : (side + 1) * 128])
    halo_copies = {id(copy) for _, copy, _ in guarded}
    for dl, copy, on in guarded:
        on(dl, False, copy.wait_send)
    for copy in copies:
        if id(copy) not in halo_copies:
            copy.wait_send()
    for copy in stores:
        copy.wait()


def per_device(
    ring,
    depth,
    inputs,
    w_reduce,
    gain_reduce,
    bias_reduce,
    w_dilated,
    gain_dilated,
    bias_dilated,
    w_expand,
    gain_expand,
    bias_expand,
    grad_out,
    labels,
    class_weight,
):
    batch, height, width, chan_in = inputs.shape
    chan_mid = w_reduce.shape[1]
    pixels = batch * height * width
    half = chan_in // 2
    terms = [
        Term(half, half, ring, depth),
        Term(5 * chan_mid, 4 * chan_mid, ring, depth),
        Term(half, half, ring, depth),
    ]
    scratch = [
        pltpu.VMEM((pixels, chan_in), BF16),
        pltpu.VMEM((chan_in, chan_mid), BF16),
        pltpu.VMEM((1, chan_mid), F32),
        pltpu.VMEM((1, chan_mid), F32),
        pltpu.VMEM((9, chan_mid, chan_mid), BF16),
        pltpu.VMEM((1, chan_mid), F32),
        pltpu.VMEM((1, chan_mid), F32),
        pltpu.VMEM((chan_mid, chan_in), BF16),
        pltpu.VMEM((1, chan_in), F32),
        pltpu.VMEM((1, chan_in), F32),
        pltpu.VMEM((pixels, chan_in), BF16),
        pltpu.VMEM((batch * width, height), jnp.int32),
        pltpu.VMEM((pixels, 1), F32),
        pltpu.VMEM((pixels, pixels), BF16),
        pltpu.VMEM((pixels, pixels), BF16),
        pltpu.VMEM((pixels, chan_mid), F32),
        pltpu.VMEM((pixels, chan_mid), F32),
        pltpu.VMEM((pixels, chan_in), F32),
        pltpu.VMEM((pixels, chan_in), BF16),
        pltpu.VMEM((height // 2 + 2, width // 2 + 2, 16, chan_mid), BF16),
        pltpu.VMEM((height // 2 + 2, width // 2 + 2, 16, chan_mid), BF16),
        pltpu.VMEM((pixels, chan_in), BF16),
    ]
    for term in terms:
        scratch += term.scratch(ring, depth)
    n_remote = 16 + 3 * (2 + 8 * (ring - 1) + 2 * (depth - 1) + 1)
    scratch += [
        pltpu.SemaphoreType.DMA((12,)),
        pltpu.SemaphoreType.DMA((2 * (chan_in // 256) + 5,)),
        pltpu.SemaphoreType.DMA((n_remote,)),
        pltpu.SemaphoreType.DMA((n_remote,)),
    ]
    anywhere = pl.BlockSpec(memory_space=pl.ANY)
    smem = pl.BlockSpec(memory_space=pltpu.SMEM)
    grad_inputs, grad_reduce, grad_dilated, grad_expand = pl.pallas_call(
        functools.partial(
            kernel, ring, depth, terms, (batch, height, width, chan_in, chan_mid)
        ),
        out_shape=(
            jax.ShapeDtypeStruct((pixels, chan_in), BF16),
            jax.ShapeDtypeStruct((chan_in, chan_mid), BF16),
            jax.ShapeDtypeStruct((9 * chan_mid, chan_mid), BF16),
            jax.ShapeDtypeStruct((chan_mid, chan_in), BF16),
        ),
        in_specs=[anywhere] * 12 + [smem],
        out_specs=(anywhere,) * 4,
        scratch_shapes=scratch,
        compiler_params=pltpu.CompilerParams(
            collective_id=0, has_side_effects=True, vmem_limit_bytes=60 * 2**20
        ),
    )(
        inputs.reshape(pixels, chan_in),
        w_reduce,
        gain_reduce.reshape(1, -1),
        bias_reduce.reshape(1, -1),
        w_dilated.reshape(9, chan_mid, chan_mid),
        gain_dilated.reshape(1, -1),
        bias_dilated.reshape(1, -1),
        w_expand,
        gain_expand.reshape(1, -1),
        bias_expand.reshape(1, -1),
        grad_out.reshape(pixels, chan_in),
        labels.transpose(0, 2, 1).reshape(batch * width, height),
        class_weight.reshape(1, -1),
    )
    return (
        grad_inputs.reshape(batch, height, width, chan_in),
        grad_reduce,
        grad_dilated.reshape(3, 3, chan_mid, chan_mid),
        grad_expand,
    )


def solution(mesh):
    ring = math.isqrt(mesh.shape["lon"] // 2)
    field = P(None, "lat", "lon", None)
    return jax.shard_map(
        functools.partial(per_device, ring, mesh.shape["lat"]),
        mesh=mesh,
        in_specs=(field,) + (P(),) * 9 + (field, P(None, "lat", "lon"), P()),
        out_specs=(field, P(), P(), P()),
        check_vma=False,
    )
```

```python
import functools
import math

import jax
import jax.numpy as jnp
from jax import lax
from jax.experimental import pallas as pl
from jax.experimental.pallas import tpu as pltpu
from jax.sharding import PartitionSpec as P

MESH = pl.DeviceIdType.MESH
F32, BF16 = jnp.float32, jnp.bfloat16


def smooth(pre):
    return pre * jax.nn.sigmoid(pre)


def slope(pre):
    sig = jax.nn.sigmoid(pre)
    return sig * (1.0 + pre * (1.0 - sig))


def dot(left, right):
    return jnp.dot(left, right, preferred_element_type=F32)


def dot_rt(left, right):
    return lax.dot_general(left, right, (((1,), (1,)), ((), ())), preferred_element_type=F32)


def dot_lt(left, right):
    return lax.dot_general(left, right, (((0,), (0,)), ((), ())), preferred_element_type=F32)


def up(n, m):
    return -(-n // m) * m


class Term:
    def __init__(self, rows_a, rows_b, ring, depth):
        self.ra, self.rb, self.rows = rows_a, rows_b, rows_a + rows_b
        self.start = (0, rows_a)
        self.part = (rows_a, rows_b)
        self.first = (rows_a // ring, rows_b // ring)
        self.second = (rows_a // ring**2, rows_b // ring**2)
        self.joined = sum(self.second)
        self.zrows = up(self.joined, 8 * depth) // depth

    def scratch(self, ring, depth):
        out = [
            pltpu.VMEM((2, self.rows, 128), BF16),
            pltpu.VMEM((self.rows, 128), BF16),
            pltpu.VMEM((self.rows, 128), BF16),
            pltpu.VMEM((self.first[0], 128), BF16),
            pltpu.VMEM((self.first[1], 128), BF16),
            pltpu.VMEM((depth * self.zrows, 128), F32),
            pltpu.VMEM((depth, self.zrows, 128), BF16),
            pltpu.VMEM((depth - 1, self.zrows, 128), BF16),
            pltpu.VMEM((self.zrows, 128), BF16),
            pltpu.VMEM((depth, self.zrows, 128), BF16),
            pltpu.VMEM((2, self.rows, 128), BF16),
        ]
        for sizes in (self.first, self.second):
            for n in sizes:
                out += [
                    pltpu.VMEM((2 * n, 128), BF16),
                    pltpu.VMEM((n, 128), F32),
                    pltpu.VMEM((n, 128), BF16),
                    pltpu.VMEM((n, 128), BF16),
                ]
        return out


def kernel(ring, depth, terms, dims, *refs):
    batch, height, width, chan_in, chan_mid = dims
    pixels = batch * height * width
    h2n, w2n = height // 2, width // 2
    lon_n = ring * ring * 2
    (x_hbm, wr_hbm, gr_hbm, br_hbm, wd_hbm, gd_hbm, bd_hbm, we_hbm, ge_hbm, be_hbm, go_hbm,
     label_hbm, class_weight,
     gi_hbm, gred_hbm, gdil_hbm, gexp_hbm,
     x_v, wr_v, gr, br, wd_v, gd, bd, we_v, ge, be, go_v, label_v,
     pw, perm, back, pre_one, slope_two, gfull, gthree, p_one, p_two, gi_v,
     *rest) = refs
    n_bufs = 27
    bufs = [rest[n_bufs * i : n_bufs * (i + 1)] for i in range(3)]
    load_sem, store_sem, send_sem, recv_sem = rest[3 * n_bufs :]

    lat, lon = lax.axis_index("lat"), lax.axis_index("lon")
    core, plane = lon % 2, lon // 2
    gx, gy = plane // ring, plane % ring

    loads = [
        pltpu.make_async_copy(src, dst, load_sem.at[i])
        for i, (src, dst) in enumerate(
            [
                (x_hbm, x_v), (wr_hbm, wr_v), (gr_hbm, gr), (br_hbm, br),
                (label_hbm, label_v), (wd_hbm, wd_v), (gd_hbm, gd), (bd_hbm, bd),
                (we_hbm, we_v), (ge_hbm, ge), (be_hbm, be), (go_hbm, go_v),
            ]
        )
    ]
    for load in loads:
        load.start()

    def at_xy(ax, ay):
        return (lat, (ax * ring + ay) * 2 + core)

    barrier = pltpu.get_barrier_semaphore()
    greet = [(lat, lon + 1 - 2 * core)]
    greet += [at_xy((gx + s) % ring, gy) for s in (1, ring - 1)]
    greet += [at_xy(gx, (gy + s) % ring) for s in (1, ring - 1)]
    greet += [((lat + s) % depth, lon) for s in range(1, depth)]
    for dl in (-1, 0, 1):
        for dw in (-1, 1):
            greet.append(((lat + dl + depth) % depth, (lon + dw + lon_n) % lon_n))
    for device in greet:
        pl.semaphore_signal(barrier, inc=1, device_id=device, device_id_type=MESH)

    def natural(p):
        return (
            ((p // 4) % batch) * (height * width)
            + (2 * (p // (16 * w2n)) + (p // 2) % 2) * width
            + 2 * ((p // 16) % w2n)
            + p % 2
        )

    lanes = lax.broadcasted_iota(jnp.int32, (pixels, 128), 1)
    rows = lax.broadcasted_iota(jnp.int32, (pixels, 128), 0)
    source = natural(lax.broadcasted_iota(jnp.int32, (pixels, 1), 0))
    for j in range(pixels // 128):
        cols = slice(j * 128, (j + 1) * 128)
        perm[:, cols] = jnp.where(source == lanes + j * 128, 1.0, 0.0).astype(BF16)
        target = natural(lax.broadcasted_iota(jnp.int32, (1, 128), 1) + j * 128)
        back[:, cols] = jnp.where(target == rows, 1.0, 0.0).astype(BF16)

    copies = []

    def remote(src, dst, device):
        i = len(copies)
        copy = pltpu.make_async_remote_copy(
            src_ref=src,
            dst_ref=dst,
            send_sem=send_sem.at[i],
            recv_sem=recv_sem.at[i],
            device_id=device,
            device_id_type=MESH,
        )
        copies.append(copy)
        return copy

    def send(src, dst, device):
        copy = remote(src, dst, device)
        copy.start()
        return copy

    guarded = []

    def halo(p_ref):
        hi, wi = slice(1, 1 + h2n), slice(1, 1 + w2n)

        @pl.when(lat == 0)
        def _():
            p_ref[0] = jnp.zeros_like(p_ref[0])

        @pl.when(lat == depth - 1)
        def _():
            p_ref[h2n + 1] = jnp.zeros_like(p_ref[h2n + 1])

        west, east = (lon + lon_n - 1) % lon_n, (lon + 1) % lon_n
        plan = []
        for dl in (0, -1, 1):
            row_src = {0: hi, -1: 1, 1: h2n}[dl]
            row_dst = {0: hi, -1: h2n + 1, 1: 0}[dl]
            there = (lat + dl + depth) % depth
            for dw in (0, -1, 1):
                if dl == 0 and dw == 0:
                    continue
                col_src = {0: wi, -1: 1, 1: w2n}[dw]
                col_dst = {0: wi, -1: w2n + 1, 1: 0}[dw]
                device = (there, {0: lon, -1: west, 1: east}[dw])
                copy = remote(p_ref.at[row_src, col_src], p_ref.at[row_dst, col_dst], device)
                plan.append((dl, copy))

        def sends(copy):
            return copy.start

        def on(dl, receiving, action):
            if dl == 0:
                action()
                return
            toward_low = (dl == -1) != receiving
            pl.when(lat > 0 if toward_low else lat < depth - 1)(action)

        for dl, copy in plan:
            on(dl, False, copy.start)
        guarded.extend((dl, copy, on) for dl, copy in plan)

        def wait():
            for dl, copy in plan:
                on(dl, True, copy.wait_recv)

        return wait

    def tap(p_ref, row, col):
        return p_ref[row : row + h2n, col : col + w2n].reshape(pixels, chan_mid)

    def to_natural(value):
        high = value.astype(BF16)
        low = (value - high.astype(F32)).astype(BF16)
        return dot(back[...], high) + dot(back[...], low)

    sibling = (lat, lon + 1 - 2 * core)

    def put_term(t, first_row, value):
        own = bufs[t][0]
        n = value.shape[0]
        own[0, first_row : first_row + n] = value[:, :128].astype(BF16)
        own[1, first_row : first_row + n] = value[:, 128:].astype(BF16)

    def core_send(t, part):
        term, b = terms[t], bufs[t]
        span = slice(term.start[part], term.start[part] + term.part[part])
        return send(b[0].at[1 - core, span], b[1].at[span], sibling)

    def halving(axis):
        at = (gx, gy)[axis]
        flip, across = at + 1 - 2 * (at % 2), ring - 1 - at
        high = (1 - core) * (((at + 1) // 2) % 2) + core * (at // 2)
        low = (1 - core) * (at // 2) + core * (at % 2)
        near = (1 - core) * flip + core * across
        far = (1 - core) * across + core * flip
        devices = [at_xy(p, gy) if axis == 0 else at_xy(gx, p) for p in (near, far)]
        return high, low, devices

    rings = [halving(0), halving(1)]

    def rows_at(start, n):
        return pl.ds(pl.multiple_of(start, 16), n)

    def reduction(t, core_copies):
        term, b = terms[t], bufs[t]

        def ring_of(part, step):
            return rings[part ^ step]

        def quarter(part, step):
            return (term.first, term.second)[step][part]

        def halves(part, step):
            at = 11 + 4 * (2 * step + part)
            return b[at : at + 4]

        def send_half(part, step, src, base):
            high, _, devices = ring_of(part, step)
            n = 2 * quarter(part, step)
            return send(src.at[rows_at(base + (1 - high) * n, n)], halves(part, step)[0], devices[0])

        def send_quarter(part, step, src, base):
            high, low, devices = ring_of(part, step)
            n = quarter(part, step)
            half, kept, sent, got = halves(part, step)
            mine = base + high * 2 * n
            for place, to in ((low, kept), (1 - low, sent)):
                value = src[rows_at(mine + place * n, n)].astype(F32)
                to[...] = (value + half[rows_at(place * n, n)].astype(F32)).astype(to.dtype)
            return send(sent, got, devices[1])

        inward = []
        for part in (0, 1):
            core_copies[part].wait_recv()
            span = slice(term.start[part], term.start[part] + term.part[part])
            b[2][span] = (b[0][core, span].astype(F32) + b[1][span].astype(F32)).astype(BF16)
            inward.append(send_half(part, 0, b[2], term.start[part]))
            yield
        sources = [(b[2], term.start[0]), (b[2], term.start[1])]
        for step in (0, 1):
            crossing = []
            for part in (0, 1):
                inward[part].wait_recv()
                crossing.append(send_quarter(part, step, *sources[part]))
            yield
            at = 0
            for part in (0, 1):
                crossing[part].wait_recv()
                _, kept, _, got = halves(part, step)
                total = kept[...] + got[...].astype(F32)
                if step == 0:
                    b[3 + part][...] = total.astype(BF16)
                    sources[part] = (b[3 + part], 0)
                    inward[part] = send_half(part, 1, *sources[part])
                else:
                    n = quarter(part, 1)
                    b[5][at : at + n] = total
                    at += n
            if step == 0:
                yield
        if at < depth * term.zrows:
            b[5][at:] = jnp.zeros((depth * term.zrows - at, 128), F32)
        b[6][...] = b[5][...].reshape(depth, term.zrows, 128).astype(BF16)
        arrived = []
        for s in range(1, depth):
            peer = (lat + s) % depth
            arrived.append(send(b[6].at[peer], b[7].at[s - 1], (peer, lon)))
        yield
        for copy in arrived:
            copy.wait_recv()
        total = b[5][pl.ds(pl.multiple_of(lat * term.zrows, 8), term.zrows)]
        for s in range(depth - 1):
            total = total + b[7][s].astype(F32)
        b[8][...] = total.astype(BF16)
        b[9][lat] = total.astype(BF16)
        arrived = [send(b[8], b[9].at[lat], ((lat + s) % depth, lon)) for s in range(1, depth)]
        yield
        for copy in arrived:
            copy.wait_recv()
        at = 0
        whole = b[9][...].astype(F32).reshape(depth * term.zrows, 128)
        final = b[10].at[core]
        base, crossing = [], []
        for part in (0, 1):
            high, low, _ = ring_of(part, 0)
            base.append(term.start[part] + (2 * high + low) * quarter(part, 0))
            high, low, devices = ring_of(part, 1)
            n = quarter(part, 1)
            here = rows_at(base[part] + (2 * high + low) * n, n)
            b[10][core, here] = whole[at : at + n].astype(BF16)
            at += n
            crossing.append(send(final.at[here], final.at[here], devices[1]))
        yield
        for step in (1, 0):
            outward = []
            for part in (0, 1):
                crossing[part].wait_recv()
                high, _, devices = ring_of(part, step)
                n = 2 * quarter(part, step)
                start = base[part] if step == 1 else term.start[part]
                here = rows_at(start + high * n, n)
                outward.append(send(final.at[here], final.at[here], devices[0]))
            yield
            crossing = []
            for part in (0, 1):
                outward[part].wait_recv()
                if step == 1:
                    here = rows_at(base[part], quarter(part, 0))
                    device = ring_of(part, 0)[2][1]
                else:
                    here = slice(term.start[part], term.start[part] + term.part[part])
                    device = sibling
                crossing.append(send(final.at[here], final.at[here], device))
            yield
        for copy in crossing:
            copy.wait_recv()
        yield

    stores = []

    def store(src, dst):
        copy = pltpu.make_async_copy(src, dst, store_sem.at[len(stores)])
        copy.start()
        stores.append(copy)

    for load in loads[:4]:
        load.wait()
    pre_one[...] = dot(x_v[...], wr_v[...]) * gr[...] + br[...]
    mid_one = smooth(pre_one[...]).astype(BF16)
    hi, wi = slice(1, 1 + h2n), slice(1, 1 + w2n)
    p_one[hi, wi] = dot(perm[...], mid_one).astype(BF16).reshape(h2n, w2n, 16, chan_mid)
    pl.semaphore_wait(barrier, len(greet))
    wait_one = halo(p_one)
    for load in loads[4:]:
        load.wait()
    lab_rows = batch * width
    pixel = lax.broadcasted_iota(jnp.int32, (pixels, lab_rows), 0)
    row = (pixel // (height * width)) * width + pixel % width
    row_hot = jnp.where(
        row == lax.broadcasted_iota(jnp.int32, (pixels, lab_rows), 1), 1.0, 0.0
    ).astype(BF16)
    picked = dot(row_hot, label_v[...].astype(F32).astype(BF16))
    pixel = lax.broadcasted_iota(jnp.int32, (pixels, height), 0)
    lane_hot = (pixel // width) % height == lax.broadcasted_iota(jnp.int32, (pixels, height), 1)
    label = jnp.sum(jnp.where(lane_hot, picked, 0.0), axis=1, keepdims=True)
    weight = class_weight[0, 0]
    for k in range(1, class_weight.shape[1]):
        weight = jnp.where(label > k - 0.5, class_weight[0, k], weight)
    pw[...] = jnp.broadcast_to(weight, pw.shape)
    total = dot(tap(p_one, 1, 1), wd_v[4])
    wait_one()
    for i in (0, 1, 2, 3, 5, 6, 7, 8):
        total = total + dot(tap(p_one, i // 3, i % 3), wd_v[i])
    pre_two = to_natural(total * gd[...] + bd[...])
    mid_two = smooth(pre_two).astype(BF16)
    slope_two[...] = slope(pre_two) * gd[...]

    blocks = chan_in // 256
    total = None
    for j in range(blocks):
        cols = slice(j * 256, (j + 1) * 256)
        w_block = we_v[:, cols]
        pre_three = dot(mid_two, w_block) * ge[:, cols] + be[:, cols] + x_v[:, cols].astype(F32)
        full = go_v[:, cols].astype(F32) * pw[...] * slope(pre_three)
        gfull[:, cols] = full
        grad_three = (full * ge[:, cols]).astype(BF16)
        gthree[:, cols] = grad_three
        term = dot_rt(grad_three, w_block)
        total = term if total is None else total + term
    grad_two = (total * slope_two[...]).astype(BF16)
    p_two[hi, wi] = dot(perm[...], grad_two).astype(BF16).reshape(h2n, w2n, 16, chan_mid)
    wait_two = halo(p_two)

    for j in range(blocks):
        put_term(0, j * 256, dot_lt(mid_two, gthree[:, j * 256 : (j + 1) * 256]))
    e_core = [core_send(0, 0), core_send(0, 1)]
    d_core, r_core = [], []
    e_sum, d_sum, r_sum = reduction(0, e_core), reduction(1, d_core), reduction(2, r_core)

    def advance(*sums):
        for gen in sums:
            next(gen)

    center = tap(p_two, 1, 1)
    taps_a = terms[1].ra // chan_mid
    for i in range(9):
        put_term(1, i * chan_mid, dot_lt(tap(p_one, i // 3, i % 3), center))
        if i == taps_a - 1:
            d_core.append(core_send(1, 0))
            advance(e_sum, e_sum)
    d_core.append(core_send(1, 1))
    advance(d_sum)

    total = dot_rt(center, wd_v[4])
    wait_two()
    for i in (0, 1, 2, 3, 5, 6, 7, 8):
        total = total + dot_rt(tap(p_two, 2 - i // 3, 2 - i % 3), wd_v[i])
        if i == 3:
            advance(d_sum, e_sum)
    grad_one = (to_natural(total) * slope(pre_one[...]) * gr[...]).astype(BF16)
    for j in range(2):
        half = chan_in // 2
        put_term(2, j * half, dot_lt(x_v[:, j * half : (j + 1) * half], grad_one))
        r_core.append(core_send(2, j))
        if j == 0:
            advance(e_sum, d_sum)
    for j in range(blocks):
        cols = slice(j * 256, (j + 1) * 256)
        gi_v[:, cols] = (dot_rt(grad_one, wr_v[cols, :]) + gfull[:, cols]).astype(BF16)
        if j == 1:
            advance(r_sum, r_sum, e_sum, d_sum)
    store(gi_v, gi_hbm)
    done = {id(e_sum): 5, id(d_sum): 4, id(r_sum): 2}
    n_stages = 13
    order = [e_sum, d_sum, r_sum]
    while any(done[id(gen)] < n_stages for gen in order):
        for gen in order:
            if done[id(gen)] < n_stages:
                advance(gen)
                done[id(gen)] += 1
                if done[id(gen)] == n_stages:
                    if gen is e_sum:
                        for side in (0, 1):
                            for j in range(blocks):
                                first = j * 256 + side * 128
                                store(
                                    bufs[0][10].at[side, j * 256 : (j + 1) * 256],
                                    gexp_hbm.at[:, first : first + 128],
                                )
                    else:
                        t, out = (1, gdil_hbm) if gen is d_sum else (2, gred_hbm)
                        for side in (0, 1):
                            store(bufs[t][10].at[side], out.at[:, side * 128 : (side + 1) * 128])
    halo_copies = {id(copy) for _, copy, _ in guarded}
    for dl, copy, on in guarded:
        on(dl, False, copy.wait_send)
    for copy in copies:
        if id(copy) not in halo_copies:
            copy.wait_send()
    for copy in stores:
        copy.wait()


def per_device(
    ring,
    depth,
    inputs,
    w_reduce,
    gain_reduce,
    bias_reduce,
    w_dilated,
    gain_dilated,
    bias_dilated,
    w_expand,
    gain_expand,
    bias_expand,
    grad_out,
    labels,
    class_weight,
):
    batch, height, width, chan_in = inputs.shape
    chan_mid = w_reduce.shape[1]
    pixels = batch * height * width
    half = chan_in // 2
    terms = [
        Term(half, half, ring, depth),
        Term(5 * chan_mid, 4 * chan_mid, ring, depth),
        Term(half, half, ring, depth),
    ]
    scratch = [
        pltpu.VMEM((pixels, chan_in), BF16),
        pltpu.VMEM((chan_in, chan_mid), BF16),
        pltpu.VMEM((1, chan_mid), F32),
        pltpu.VMEM((1, chan_mid), F32),
        pltpu.VMEM((9, chan_mid, chan_mid), BF16),
        pltpu.VMEM((1, chan_mid), F32),
        pltpu.VMEM((1, chan_mid), F32),
        pltpu.VMEM((chan_mid, chan_in), BF16),
        pltpu.VMEM((1, chan_in), F32),
        pltpu.VMEM((1, chan_in), F32),
        pltpu.VMEM((pixels, chan_in), BF16),
        pltpu.VMEM((batch * width, height), jnp.int32),
        pltpu.VMEM((pixels, 1), F32),
        pltpu.VMEM((pixels, pixels), BF16),
        pltpu.VMEM((pixels, pixels), BF16),
        pltpu.VMEM((pixels, chan_mid), F32),
        pltpu.VMEM((pixels, chan_mid), F32),
        pltpu.VMEM((pixels, chan_in), F32),
        pltpu.VMEM((pixels, chan_in), BF16),
        pltpu.VMEM((height // 2 + 2, width // 2 + 2, 16, chan_mid), BF16),
        pltpu.VMEM((height // 2 + 2, width // 2 + 2, 16, chan_mid), BF16),
        pltpu.VMEM((pixels, chan_in), BF16),
    ]
    for term in terms:
        scratch += term.scratch(ring, depth)
    n_remote = 16 + 3 * (2 + 8 * (ring - 1) + 2 * (depth - 1) + 1)
    scratch += [
        pltpu.SemaphoreType.DMA((12,)),
        pltpu.SemaphoreType.DMA((2 * (chan_in // 256) + 5,)),
        pltpu.SemaphoreType.DMA((n_remote,)),
        pltpu.SemaphoreType.DMA((n_remote,)),
    ]
    anywhere = pl.BlockSpec(memory_space=pl.ANY)
    smem = pl.BlockSpec(memory_space=pltpu.SMEM)
    grad_inputs, grad_reduce, grad_dilated, grad_expand = pl.pallas_call(
        functools.partial(
            kernel, ring, depth, terms, (batch, height, width, chan_in, chan_mid)
        ),
        out_shape=(
            jax.ShapeDtypeStruct((pixels, chan_in), BF16),
            jax.ShapeDtypeStruct((chan_in, chan_mid), BF16),
            jax.ShapeDtypeStruct((9 * chan_mid, chan_mid), BF16),
            jax.ShapeDtypeStruct((chan_mid, chan_in), BF16),
        ),
        in_specs=[anywhere] * 12 + [smem],
        out_specs=(anywhere,) * 4,
        scratch_shapes=scratch,
        compiler_params=pltpu.CompilerParams(
            collective_id=0, has_side_effects=True, vmem_limit_bytes=60 * 2**20
        ),
    )(
        inputs.reshape(pixels, chan_in),
        w_reduce,
        gain_reduce.reshape(1, -1),
        bias_reduce.reshape(1, -1),
        w_dilated.reshape(9, chan_mid, chan_mid),
        gain_dilated.reshape(1, -1),
        bias_dilated.reshape(1, -1),
        w_expand,
        gain_expand.reshape(1, -1),
        bias_expand.reshape(1, -1),
        grad_out.reshape(pixels, chan_in),
        labels.transpose(0, 2, 1).reshape(batch * width, height),
        class_weight.reshape(1, -1),
    )
    return (
        grad_inputs.reshape(batch, height, width, chan_in),
        grad_reduce,
        grad_dilated.reshape(3, 3, chan_mid, chan_mid),
        grad_expand,
    )


def solution(mesh):
    ring = math.isqrt(mesh.shape["lon"] // 2)
    field = P(None, "lat", "lon", None)
    return jax.shard_map(
        functools.partial(per_device, ring, mesh.shape["lat"]),
        mesh=mesh,
        in_specs=(field,) + (P(),) * 9 + (field, P(None, "lat", "lon"), P()),
        out_specs=(field, P(), P(), P()),
        check_vma=False,
    )
```

```python
import functools
import math

import jax
import jax.numpy as jnp
from jax import lax
from jax.experimental import pallas as pl
from jax.experimental.pallas import tpu as pltpu
from jax.sharding import PartitionSpec as P

MESH = pl.DeviceIdType.MESH
F32, BF16 = jnp.float32, jnp.bfloat16


def smooth(pre):
    return pre * jax.nn.sigmoid(pre)


def slope(pre):
    sig = jax.nn.sigmoid(pre)
    return sig * (1.0 + pre * (1.0 - sig))


def dot(left, right):
    return jnp.dot(left, right, preferred_element_type=F32)


def dot_rt(left, right):
    return lax.dot_general(left, right, (((1,), (1,)), ((), ())), preferred_element_type=F32)


def dot_lt(left, right):
    return lax.dot_general(left, right, (((0,), (0,)), ((), ())), preferred_element_type=F32)


def up(n, m):
    return -(-n // m) * m


class Term:
    def __init__(self, rows_a, rows_b, ring, depth):
        self.ra, self.rb, self.rows = rows_a, rows_b, rows_a + rows_b
        self.start = (0, rows_a)
        self.part = (rows_a, rows_b)
        self.first = (rows_a // ring, rows_b // ring)
        self.second = (rows_a // ring**2, rows_b // ring**2)
        self.joined = sum(self.second)
        self.zrows = up(self.joined, 8 * depth) // depth

    def scratch(self, ring, depth):
        return [
            pltpu.VMEM((2, self.rows, 128), BF16),
            pltpu.VMEM((self.rows, 128), BF16),
            pltpu.VMEM((self.rows, 128), BF16),
            pltpu.VMEM((ring - 1, self.first[0], 128), BF16),
            pltpu.VMEM((ring - 1, self.first[1], 128), BF16),
            pltpu.VMEM((self.first[0], 128), BF16),
            pltpu.VMEM((self.first[1], 128), BF16),
            pltpu.VMEM((ring - 1, self.second[0], 128), BF16),
            pltpu.VMEM((ring - 1, self.second[1], 128), BF16),
            pltpu.VMEM((depth * self.zrows, 128), F32),
            pltpu.VMEM((depth - 1, self.zrows, 128), BF16),
            pltpu.VMEM((self.zrows, 128), BF16),
            pltpu.VMEM((depth, self.zrows, 128), BF16),
            pltpu.VMEM((2, self.rows, 128), BF16),
            pltpu.VMEM((depth, self.zrows, 128), BF16),
        ]


def kernel(ring, depth, terms, dims, *refs):
    batch, height, width, chan_in, chan_mid = dims
    pixels = batch * height * width
    h2n, w2n = height // 2, width // 2
    lon_n = ring * ring * 2
    (x_hbm, wr_hbm, gr_hbm, br_hbm, wd_hbm, gd_hbm, bd_hbm, we_hbm, ge_hbm, be_hbm, go_hbm,
     label_hbm, class_weight,
     gi_hbm, gred_hbm, gdil_hbm, gexp_hbm,
     x_v, wr_v, gr, br, wd_v, gd, bd, we_v, ge, be, go_v, label_v,
     pw, perm, back, pre_one, slope_two, gfull, gthree, p_one, p_two, gi_v,
     *rest) = refs
    n_bufs = 15
    bufs = [rest[n_bufs * i : n_bufs * (i + 1)] for i in range(3)]
    load_sem, store_sem, send_sem, recv_sem = rest[3 * n_bufs :]

    lat, lon = lax.axis_index("lat"), lax.axis_index("lon")
    core, plane = lon % 2, lon // 2
    gx, gy = plane // ring, plane % ring

    loads = [
        pltpu.make_async_copy(src, dst, load_sem.at[i])
        for i, (src, dst) in enumerate(
            [
                (x_hbm, x_v), (wr_hbm, wr_v), (gr_hbm, gr), (br_hbm, br),
                (label_hbm, label_v), (wd_hbm, wd_v), (gd_hbm, gd), (bd_hbm, bd),
                (we_hbm, we_v), (ge_hbm, ge), (be_hbm, be), (go_hbm, go_v),
            ]
        )
    ]
    for load in loads:
        load.start()

    def at_xy(ax, ay):
        return (lat, (ax * ring + ay) * 2 + core)

    barrier = pltpu.get_barrier_semaphore()
    greet = [(lat, lon + 1 - 2 * core)]
    greet += [at_xy((gx + s) % ring, gy) for s in range(1, ring)]
    greet += [at_xy(gx, (gy + s) % ring) for s in range(1, ring)]
    greet += [((lat + s) % depth, lon) for s in range(1, depth)]
    for dl in (-1, 0, 1):
        for dw in (-1, 1):
            greet.append(((lat + dl + depth) % depth, (lon + dw + lon_n) % lon_n))
    for device in greet:
        pl.semaphore_signal(barrier, inc=1, device_id=device, device_id_type=MESH)

    def natural(p):
        return (
            ((p // 4) % batch) * (height * width)
            + (2 * (p // (16 * w2n)) + (p // 2) % 2) * width
            + 2 * ((p // 16) % w2n)
            + p % 2
        )

    lanes = lax.broadcasted_iota(jnp.int32, (pixels, 128), 1)
    rows = lax.broadcasted_iota(jnp.int32, (pixels, 128), 0)
    source = natural(lax.broadcasted_iota(jnp.int32, (pixels, 1), 0))
    for j in range(pixels // 128):
        cols = slice(j * 128, (j + 1) * 128)
        perm[:, cols] = jnp.where(source == lanes + j * 128, 1.0, 0.0).astype(BF16)
        target = natural(lax.broadcasted_iota(jnp.int32, (1, 128), 1) + j * 128)
        back[:, cols] = jnp.where(target == rows, 1.0, 0.0).astype(BF16)

    copies = []

    def remote(src, dst, device):
        i = len(copies)
        copy = pltpu.make_async_remote_copy(
            src_ref=src,
            dst_ref=dst,
            send_sem=send_sem.at[i],
            recv_sem=recv_sem.at[i],
            device_id=device,
            device_id_type=MESH,
        )
        copies.append(copy)
        return copy

    def send(src, dst, device):
        copy = remote(src, dst, device)
        copy.start()
        return copy

    guarded = []

    def halo(p_ref):
        hi, wi = slice(1, 1 + h2n), slice(1, 1 + w2n)

        @pl.when(lat == 0)
        def _():
            p_ref[0] = jnp.zeros_like(p_ref[0])

        @pl.when(lat == depth - 1)
        def _():
            p_ref[h2n + 1] = jnp.zeros_like(p_ref[h2n + 1])

        west, east = (lon + lon_n - 1) % lon_n, (lon + 1) % lon_n
        plan = []
        for dl in (0, -1, 1):
            row_src = {0: hi, -1: 1, 1: h2n}[dl]
            row_dst = {0: hi, -1: h2n + 1, 1: 0}[dl]
            there = (lat + dl + depth) % depth
            for dw in (0, -1, 1):
                if dl == 0 and dw == 0:
                    continue
                col_src = {0: wi, -1: 1, 1: w2n}[dw]
                col_dst = {0: wi, -1: w2n + 1, 1: 0}[dw]
                device = (there, {0: lon, -1: west, 1: east}[dw])
                copy = remote(p_ref.at[row_src, col_src], p_ref.at[row_dst, col_dst], device)
                plan.append((dl, copy))

        def sends(copy):
            return copy.start

        def on(dl, receiving, action):
            if dl == 0:
                action()
                return
            toward_low = (dl == -1) != receiving
            pl.when(lat > 0 if toward_low else lat < depth - 1)(action)

        for dl, copy in plan:
            on(dl, False, copy.start)
        guarded.extend((dl, copy, on) for dl, copy in plan)

        def wait():
            for dl, copy in plan:
                on(dl, True, copy.wait_recv)

        return wait

    def tap(p_ref, row, col):
        return p_ref[row : row + h2n, col : col + w2n].reshape(pixels, chan_mid)

    def to_natural(value):
        high = value.astype(BF16)
        low = (value - high.astype(F32)).astype(BF16)
        return dot(back[...], high) + dot(back[...], low)

    sibling = (lat, lon + 1 - 2 * core)

    def put_term(t, first_row, value):
        own = bufs[t][0]
        n = value.shape[0]
        own[0, first_row : first_row + n] = value[:, :128].astype(BF16)
        own[1, first_row : first_row + n] = value[:, 128:].astype(BF16)

    def core_send(t, part):
        term, b = terms[t], bufs[t]
        span = slice(term.start[part], term.start[part] + term.part[part])
        return send(b[0].at[1 - core, span], b[1].at[span], sibling)

    def ring_pos(part, step):
        return (gx, gy)[part ^ step]

    def ring_dev(part, step, s):
        if part ^ step == 0:
            return at_xy((gx + s) % ring, gy)
        return at_xy(gx, (gy + s) % ring)

    def pair_and_first(t, part, arrived):
        term, b = terms[t], bufs[t]
        arrived.wait_recv()
        lo, n = term.start[part], term.part[part]
        span = slice(lo, lo + n)
        b[2][span] = (b[0][core, span].astype(F32) + b[1][span].astype(F32)).astype(BF16)
        step = term.first[part]
        out = []
        for s in range(1, ring):
            peer = (ring_pos(part, 0) + s) % ring
            src = b[2].at[pl.ds(pl.multiple_of(lo + peer * step, 16), step)]
            out.append(send(src, b[3 + part].at[s - 1], ring_dev(part, 0, s)))
        return out

    def second(t, part, arrived):
        term, b = terms[t], bufs[t]
        for copy in arrived:
            copy.wait_recv()
        lo, n = term.start[part], term.first[part]
        mine = pl.ds(pl.multiple_of(lo + ring_pos(part, 0) * n, 16), n)
        total = b[2][mine].astype(F32)
        for s in range(ring - 1):
            total = total + b[3 + part][s].astype(F32)
        b[5 + part][...] = total.astype(BF16)
        step = term.second[part]
        out = []
        for s in range(1, ring):
            peer = (ring_pos(part, 1) + s) % ring
            src = b[5 + part].at[pl.ds(pl.multiple_of(peer * step, 16), step)]
            out.append(send(src, b[7 + part].at[s - 1], ring_dev(part, 1, s)))
        return out

    def third(t, arrived):
        term, b = terms[t], bufs[t]
        at = 0
        for part in (0, 1):
            for copy in arrived[part]:
                copy.wait_recv()
            n = term.second[part]
            mine = pl.ds(pl.multiple_of(ring_pos(part, 1) * n, 16), n)
            total = b[5 + part][mine].astype(F32)
            for s in range(ring - 1):
                total = total + b[7 + part][s].astype(F32)
            b[9][at : at + n] = total
            at += n
        if at < depth * term.zrows:
            b[9][at:] = jnp.zeros((depth * term.zrows - at, 128), F32)
        b[14][...] = b[9][...].reshape(depth, term.zrows, 128).astype(BF16)
        out = []
        for s in range(1, depth):
            peer = (lat + s) % depth
            out.append(send(b[14].at[peer], b[10].at[s - 1], (peer, lon)))
        return out

    def fourth(t, arrived):
        term, b = terms[t], bufs[t]
        for copy in arrived:
            copy.wait_recv()
        mine = pl.ds(pl.multiple_of(lat * term.zrows, 8), term.zrows)
        total = b[9][mine]
        for s in range(depth - 1):
            total = total + b[10][s].astype(F32)
        b[11][...] = total.astype(BF16)
        b[12][lat] = total.astype(BF16)
        return [
            send(b[11], b[12].at[lat], ((lat + s) % depth, lon)) for s in range(1, depth)
        ]

    def fifth(t, arrived):
        term, b = terms[t], bufs[t]
        for copy in arrived:
            copy.wait_recv()
        at, outs = 0, []
        whole = b[12][...].astype(F32).reshape(depth * term.zrows, 128)
        for part in (0, 1):
            n = term.second[part]
            place = term.start[part] + ring_pos(part, 0) * term.first[part] + ring_pos(part, 1) * n
            here = pl.ds(pl.multiple_of(place, 16), n)
            b[13][core, here] = whole[at : at + n].astype(BF16)
            at += n
            block = b[13].at[core, here]
            outs.append([send(block, block, ring_dev(part, 1, s)) for s in range(1, ring)])
        return outs

    def sixth(t, arrived):
        term, b = terms[t], bufs[t]
        outs, across = [], []
        for part in (0, 1):
            for copy in arrived[part]:
                copy.wait_recv()
            n = term.first[part]
            place = term.start[part] + ring_pos(part, 0) * n
            block = b[13].at[core, pl.ds(pl.multiple_of(place, 16), n)]
            outs.append([send(block, block, ring_dev(part, 0, s)) for s in range(1, ring)])
            across.append(send(block, block, sibling))
        return outs, across

    def seventh(t, arrived, out, blocks):
        term, b = terms[t], bufs[t]
        outs, across = arrived
        for s in range(1, ring):
            for part in (0, 1):
                outs[part][s - 1].wait_recv()
                n = term.first[part]
                place = term.start[part] + ((ring_pos(part, 0) + ring - s) % ring) * n
                block = b[13].at[core, pl.ds(pl.multiple_of(place, 16), n)]
                across.append(send(block, block, sibling))
        store_side(t, core, out, blocks)
        return across

    def last(t, across, out, blocks):
        for copy in across:
            copy.wait_recv()
        store_side(t, 1 - core, out, blocks)

    def store_side(t, side, out, blocks):
        rows = terms[t].rows // blocks
        for j in range(blocks):
            cols = pl.ds(pl.multiple_of(j * 256 + side * 128, 128), 128)
            store(bufs[t][13].at[side, j * rows : (j + 1) * rows], out.at[:, cols])

    stores = []

    def store(src, dst):
        copy = pltpu.make_async_copy(src, dst, store_sem.at[len(stores)])
        copy.start()
        stores.append(copy)

    for load in loads[:4]:
        load.wait()
    pre_one[...] = dot(x_v[...], wr_v[...]) * gr[...] + br[...]
    mid_one = smooth(pre_one[...]).astype(BF16)
    hi, wi = slice(1, 1 + h2n), slice(1, 1 + w2n)
    p_one[hi, wi] = dot(perm[...], mid_one).astype(BF16).reshape(h2n, w2n, 16, chan_mid)
    pl.semaphore_wait(barrier, len(greet))
    wait_one = halo(p_one)
    for load in loads[4:]:
        load.wait()
    lab_rows = batch * width
    pixel = lax.broadcasted_iota(jnp.int32, (pixels, lab_rows), 0)
    row = (pixel // (height * width)) * width + pixel % width
    row_hot = jnp.where(
        row == lax.broadcasted_iota(jnp.int32, (pixels, lab_rows), 1), 1.0, 0.0
    ).astype(BF16)
    picked = dot(row_hot, label_v[...].astype(F32).astype(BF16))
    pixel = lax.broadcasted_iota(jnp.int32, (pixels, height), 0)
    lane_hot = (pixel // width) % height == lax.broadcasted_iota(jnp.int32, (pixels, height), 1)
    label = jnp.sum(jnp.where(lane_hot, picked, 0.0), axis=1, keepdims=True)
    weight = class_weight[0, 0]
    for k in range(1, class_weight.shape[1]):
        weight = jnp.where(label > k - 0.5, class_weight[0, k], weight)
    pw[...] = jnp.broadcast_to(weight, pw.shape)
    total = dot(tap(p_one, 1, 1), wd_v[4])
    wait_one()
    for i in (0, 1, 2, 3, 5, 6, 7, 8):
        total = total + dot(tap(p_one, i // 3, i % 3), wd_v[i])
    pre_two = to_natural(total * gd[...] + bd[...])
    mid_two = smooth(pre_two).astype(BF16)
    slope_two[...] = slope(pre_two) * gd[...]

    blocks = chan_in // 256
    total = None
    for j in range(blocks):
        cols = slice(j * 256, (j + 1) * 256)
        w_block = we_v[:, cols]
        pre_three = dot(mid_two, w_block) * ge[:, cols] + be[:, cols] + x_v[:, cols].astype(F32)
        full = go_v[:, cols].astype(F32) * pw[...] * slope(pre_three)
        gfull[:, cols] = full
        grad_three = (full * ge[:, cols]).astype(BF16)
        gthree[:, cols] = grad_three
        term = dot_rt(grad_three, w_block)
        total = term if total is None else total + term
    grad_two = (total * slope_two[...]).astype(BF16)
    p_two[hi, wi] = dot(perm[...], grad_two).astype(BF16).reshape(h2n, w2n, 16, chan_mid)
    wait_two = halo(p_two)

    for j in range(blocks):
        put_term(0, j * 256, dot_lt(mid_two, gthree[:, j * 256 : (j + 1) * 256]))
    e_core = [core_send(0, 0), core_send(0, 1)]
    center = tap(p_two, 1, 1)
    taps_a = terms[1].ra // chan_mid
    d_core = []
    for i in range(9):
        put_term(1, i * chan_mid, dot_lt(tap(p_one, i // 3, i % 3), center))
        if i == taps_a - 1:
            d_core.append(core_send(1, 0))
            e_first = [pair_and_first(0, part, e_core[part]) for part in (0, 1)]
    d_core.append(core_send(1, 1))

    total = dot_rt(center, wd_v[4])
    wait_two()
    for i in (0, 1, 2, 3, 5, 6, 7, 8):
        total = total + dot_rt(tap(p_two, 2 - i // 3, 2 - i % 3), wd_v[i])
    grad_one = (to_natural(total) * slope(pre_one[...]) * gr[...]).astype(BF16)
    r_core = []
    for j in range(2):
        half = chan_in // 2
        put_term(2, j * half, dot_lt(x_v[:, j * half : (j + 1) * half], grad_one))
        r_core.append(core_send(2, j))
    d_first = [pair_and_first(1, part, d_core[part]) for part in (0, 1)]
    e_second = [second(0, part, e_first[part]) for part in (0, 1)]

    def input_grad(j):
        cols = slice(j * 256, (j + 1) * 256)
        gi_v[:, cols] = (dot_rt(grad_one, wr_v[cols, :]) + gfull[:, cols]).astype(BF16)

    input_grad(0)
    r_first = [pair_and_first(2, part, r_core[part]) for part in (0, 1)]
    e_third = third(0, e_second)
    input_grad(1)
    d_second = [second(1, part, d_first[part]) for part in (0, 1)]
    for j in range(2, blocks):
        input_grad(j)
    store(gi_v, gi_hbm)
    r_second = [second(2, part, r_first[part]) for part in (0, 1)]
    d_third = third(1, d_second)
    e_fourth = fourth(0, e_third)
    r_third = third(2, r_second)
    d_fourth = fourth(1, d_third)
    e_fifth = fifth(0, e_fourth)
    r_fourth = fourth(2, r_third)
    d_fifth = fifth(1, d_fourth)
    e_sixth = sixth(0, e_fifth)
    r_fifth = fifth(2, r_fourth)
    d_sixth = sixth(1, d_fifth)
    e_last = seventh(0, e_sixth, gexp_hbm, blocks)
    r_sixth = sixth(2, r_fifth)
    d_last = seventh(1, d_sixth, gdil_hbm, 1)
    last(0, e_last, gexp_hbm, blocks)
    r_last = seventh(2, r_sixth, gred_hbm, 1)
    last(1, d_last, gdil_hbm, 1)
    last(2, r_last, gred_hbm, 1)
    halo_copies = {id(copy) for _, copy, _ in guarded}
    for dl, copy, on in guarded:
        on(dl, False, copy.wait_send)
    for copy in copies:
        if id(copy) not in halo_copies:
            copy.wait_send()
    for copy in stores:
        copy.wait()


def per_device(
    ring,
    depth,
    inputs,
    w_reduce,
    gain_reduce,
    bias_reduce,
    w_dilated,
    gain_dilated,
    bias_dilated,
    w_expand,
    gain_expand,
    bias_expand,
    grad_out,
    labels,
    class_weight,
):
    batch, height, width, chan_in = inputs.shape
    chan_mid = w_reduce.shape[1]
    pixels = batch * height * width
    half = chan_in // 2
    terms = [
        Term(half, half, ring, depth),
        Term(5 * chan_mid, 4 * chan_mid, ring, depth),
        Term(half, half, ring, depth),
    ]
    scratch = [
        pltpu.VMEM((pixels, chan_in), BF16),
        pltpu.VMEM((chan_in, chan_mid), BF16),
        pltpu.VMEM((1, chan_mid), F32),
        pltpu.VMEM((1, chan_mid), F32),
        pltpu.VMEM((9, chan_mid, chan_mid), BF16),
        pltpu.VMEM((1, chan_mid), F32),
        pltpu.VMEM((1, chan_mid), F32),
        pltpu.VMEM((chan_mid, chan_in), BF16),
        pltpu.VMEM((1, chan_in), F32),
        pltpu.VMEM((1, chan_in), F32),
        pltpu.VMEM((pixels, chan_in), BF16),
        pltpu.VMEM((batch * width, height), jnp.int32),
        pltpu.VMEM((pixels, 1), F32),
        pltpu.VMEM((pixels, pixels), BF16),
        pltpu.VMEM((pixels, pixels), BF16),
        pltpu.VMEM((pixels, chan_mid), F32),
        pltpu.VMEM((pixels, chan_mid), F32),
        pltpu.VMEM((pixels, chan_in), F32),
        pltpu.VMEM((pixels, chan_in), BF16),
        pltpu.VMEM((height // 2 + 2, width // 2 + 2, 16, chan_mid), BF16),
        pltpu.VMEM((height // 2 + 2, width // 2 + 2, 16, chan_mid), BF16),
        pltpu.VMEM((pixels, chan_in), BF16),
    ]
    for term in terms:
        scratch += term.scratch(ring, depth)
    n_remote = 16 + 3 * (2 + 8 * (ring - 1) + 2 * (depth - 1) + 2 * ring)
    scratch += [
        pltpu.SemaphoreType.DMA((12,)),
        pltpu.SemaphoreType.DMA((2 * (chan_in // 256) + 5,)),
        pltpu.SemaphoreType.DMA((n_remote,)),
        pltpu.SemaphoreType.DMA((n_remote,)),
    ]
    anywhere = pl.BlockSpec(memory_space=pl.ANY)
    smem = pl.BlockSpec(memory_space=pltpu.SMEM)
    grad_inputs, grad_reduce, grad_dilated, grad_expand = pl.pallas_call(
        functools.partial(
            kernel, ring, depth, terms, (batch, height, width, chan_in, chan_mid)
        ),
        out_shape=(
            jax.ShapeDtypeStruct((pixels, chan_in), BF16),
            jax.ShapeDtypeStruct((chan_in, chan_mid), BF16),
            jax.ShapeDtypeStruct((9 * chan_mid, chan_mid), BF16),
            jax.ShapeDtypeStruct((chan_mid, chan_in), BF16),
        ),
        in_specs=[anywhere] * 12 + [smem],
        out_specs=(anywhere,) * 4,
        scratch_shapes=scratch,
        compiler_params=pltpu.CompilerParams(
            collective_id=0, has_side_effects=True, vmem_limit_bytes=60 * 2**20
        ),
    )(
        inputs.reshape(pixels, chan_in),
        w_reduce,
        gain_reduce.reshape(1, -1),
        bias_reduce.reshape(1, -1),
        w_dilated.reshape(9, chan_mid, chan_mid),
        gain_dilated.reshape(1, -1),
        bias_dilated.reshape(1, -1),
        w_expand,
        gain_expand.reshape(1, -1),
        bias_expand.reshape(1, -1),
        grad_out.reshape(pixels, chan_in),
        labels.transpose(0, 2, 1).reshape(batch * width, height),
        class_weight.reshape(1, -1),
    )
    return (
        grad_inputs.reshape(batch, height, width, chan_in),
        grad_reduce,
        grad_dilated.reshape(3, 3, chan_mid, chan_mid),
        grad_expand,
    )


def solution(mesh):
    ring = math.isqrt(mesh.shape["lon"] // 2)
    field = P(None, "lat", "lon", None)
    return jax.shard_map(
        functools.partial(per_device, ring, mesh.shape["lat"]),
        mesh=mesh,
        in_specs=(field,) + (P(),) * 9 + (field, P(None, "lat", "lon"), P()),
        out_specs=(field, P(), P(), P()),
        check_vma=False,
    )
```

```python
import functools
import math

import jax
import jax.numpy as jnp
from jax import lax
from jax.experimental import pallas as pl
from jax.experimental.pallas import tpu as pltpu
from jax.sharding import PartitionSpec as P

MESH = pl.DeviceIdType.MESH
F32, BF16 = jnp.float32, jnp.bfloat16


def smooth(pre):
    return pre * jax.nn.sigmoid(pre)


def slope(pre):
    sig = jax.nn.sigmoid(pre)
    return sig * (1.0 + pre * (1.0 - sig))


def dot(left, right):
    return jnp.dot(left, right, preferred_element_type=F32)


def dot_rt(left, right):
    return lax.dot_general(left, right, (((1,), (1,)), ((), ())), preferred_element_type=F32)


def dot_lt(left, right):
    return lax.dot_general(left, right, (((0,), (0,)), ((), ())), preferred_element_type=F32)


def up(n, m):
    return -(-n // m) * m


class Term:
    def __init__(self, rows_a, rows_b, ring, depth):
        self.ra, self.rb, self.rows = rows_a, rows_b, rows_a + rows_b
        self.start = (0, rows_a)
        self.part = (rows_a, rows_b)
        self.first = (rows_a // ring, rows_b // ring)
        self.second = (rows_a // ring**2, rows_b // ring**2)
        self.joined = sum(self.second)
        self.zrows = up(self.joined, 8 * depth) // depth

    def scratch(self, ring, depth):
        return [
            pltpu.VMEM((2, self.rows, 128), BF16),
            pltpu.VMEM((self.rows, 128), BF16),
            pltpu.VMEM((self.rows, 128), BF16),
            pltpu.VMEM((ring - 1, self.first[0], 128), BF16),
            pltpu.VMEM((ring - 1, self.first[1], 128), BF16),
            pltpu.VMEM((self.first[0], 128), BF16),
            pltpu.VMEM((self.first[1], 128), BF16),
            pltpu.VMEM((ring - 1, self.second[0], 128), BF16),
            pltpu.VMEM((ring - 1, self.second[1], 128), BF16),
            pltpu.VMEM((depth * self.zrows, 128), F32),
            pltpu.VMEM((depth - 1, self.zrows, 128), BF16),
            pltpu.VMEM((self.zrows, 128), BF16),
            pltpu.VMEM((depth, self.zrows, 128), BF16),
            pltpu.VMEM((2, self.rows, 128), BF16),
            pltpu.VMEM((depth, self.zrows, 128), BF16),
        ]


def kernel(ring, depth, terms, dims, *refs):
    batch, height, width, chan_in, chan_mid = dims
    pixels = batch * height * width
    h2n, w2n = height // 2, width // 2
    lon_n = ring * ring * 2
    (x_hbm, wr_hbm, gr_hbm, br_hbm, wd_hbm, gd_hbm, bd_hbm, we_hbm, ge_hbm, be_hbm, go_hbm,
     label_hbm, class_weight,
     gi_hbm, gred_hbm, gdil_hbm, gexp_hbm,
     x_v, wr_v, gr, br, wd_v, gd, bd, we_v, ge, be, go_v, label_v,
     pw, perm, back, pre_one, slope_two, gfull, gthree, p_one, p_two, gi_v,
     *rest) = refs
    n_bufs = 15
    bufs = [rest[n_bufs * i : n_bufs * (i + 1)] for i in range(3)]
    load_sem, store_sem, send_sem, recv_sem = rest[3 * n_bufs :]

    lat, lon = lax.axis_index("lat"), lax.axis_index("lon")
    core, plane = lon % 2, lon // 2
    gx, gy = plane // ring, plane % ring

    loads = [
        pltpu.make_async_copy(src, dst, load_sem.at[i])
        for i, (src, dst) in enumerate(
            [
                (x_hbm, x_v), (wr_hbm, wr_v), (gr_hbm, gr), (br_hbm, br),
                (label_hbm, label_v), (wd_hbm, wd_v), (gd_hbm, gd), (bd_hbm, bd),
                (we_hbm, we_v), (ge_hbm, ge), (be_hbm, be), (go_hbm, go_v),
            ]
        )
    ]
    for load in loads:
        load.start()

    def at_xy(ax, ay):
        return (lat, (ax * ring + ay) * 2 + core)

    barrier = pltpu.get_barrier_semaphore()
    greet = [(lat, lon + 1 - 2 * core)]
    greet += [at_xy((gx + s) % ring, gy) for s in range(1, ring)]
    greet += [at_xy(gx, (gy + s) % ring) for s in range(1, ring)]
    greet += [((lat + s) % depth, lon) for s in range(1, depth)]
    for dl in (-1, 0, 1):
        for dw in (-1, 1):
            greet.append(((lat + dl + depth) % depth, (lon + dw + lon_n) % lon_n))
    for device in greet:
        pl.semaphore_signal(barrier, inc=1, device_id=device, device_id_type=MESH)

    def natural(p):
        return (
            ((p // 4) % batch) * (height * width)
            + (2 * (p // (16 * w2n)) + (p // 2) % 2) * width
            + 2 * ((p // 16) % w2n)
            + p % 2
        )

    lanes = lax.broadcasted_iota(jnp.int32, (pixels, 128), 1)
    rows = lax.broadcasted_iota(jnp.int32, (pixels, 128), 0)
    source = natural(lax.broadcasted_iota(jnp.int32, (pixels, 1), 0))
    for j in range(pixels // 128):
        cols = slice(j * 128, (j + 1) * 128)
        perm[:, cols] = jnp.where(source == lanes + j * 128, 1.0, 0.0).astype(BF16)
        target = natural(lax.broadcasted_iota(jnp.int32, (1, 128), 1) + j * 128)
        back[:, cols] = jnp.where(target == rows, 1.0, 0.0).astype(BF16)

    copies = []

    def remote(src, dst, device):
        i = len(copies)
        copy = pltpu.make_async_remote_copy(
            src_ref=src,
            dst_ref=dst,
            send_sem=send_sem.at[i],
            recv_sem=recv_sem.at[i],
            device_id=device,
            device_id_type=MESH,
        )
        copies.append(copy)
        return copy

    def send(src, dst, device):
        copy = remote(src, dst, device)
        copy.start()
        return copy

    guarded = []

    def halo(p_ref):
        hi, wi = slice(1, 1 + h2n), slice(1, 1 + w2n)

        @pl.when(lat == 0)
        def _():
            p_ref[0] = jnp.zeros_like(p_ref[0])

        @pl.when(lat == depth - 1)
        def _():
            p_ref[h2n + 1] = jnp.zeros_like(p_ref[h2n + 1])

        west, east = (lon + lon_n - 1) % lon_n, (lon + 1) % lon_n
        plan = []
        for dl in (0, -1, 1):
            row_src = {0: hi, -1: 1, 1: h2n}[dl]
            row_dst = {0: hi, -1: h2n + 1, 1: 0}[dl]
            there = (lat + dl + depth) % depth
            for dw in (0, -1, 1):
                if dl == 0 and dw == 0:
                    continue
                col_src = {0: wi, -1: 1, 1: w2n}[dw]
                col_dst = {0: wi, -1: w2n + 1, 1: 0}[dw]
                device = (there, {0: lon, -1: west, 1: east}[dw])
                copy = remote(p_ref.at[row_src, col_src], p_ref.at[row_dst, col_dst], device)
                plan.append((dl, copy))

        def sends(copy):
            return copy.start

        def on(dl, receiving, action):
            if dl == 0:
                action()
                return
            toward_low = (dl == -1) != receiving
            pl.when(lat > 0 if toward_low else lat < depth - 1)(action)

        for dl, copy in plan:
            on(dl, False, copy.start)
        guarded.extend((dl, copy, on) for dl, copy in plan)

        def wait():
            for dl, copy in plan:
                on(dl, True, copy.wait_recv)

        return wait

    def tap(p_ref, row, col):
        return p_ref[row : row + h2n, col : col + w2n].reshape(pixels, chan_mid)

    def to_natural(value):
        high = value.astype(BF16)
        low = (value - high.astype(F32)).astype(BF16)
        return dot(back[...], high) + dot(back[...], low)

    sibling = (lat, lon + 1 - 2 * core)

    def put_term(t, first_row, value):
        own = bufs[t][0]
        n = value.shape[0]
        own[0, first_row : first_row + n] = value[:, :128].astype(BF16)
        own[1, first_row : first_row + n] = value[:, 128:].astype(BF16)

    def core_send(t, part):
        term, b = terms[t], bufs[t]
        span = slice(term.start[part], term.start[part] + term.part[part])
        return send(b[0].at[1 - core, span], b[1].at[span], sibling)

    def ring_pos(part, step):
        return (gx, gy)[part ^ step]

    def ring_dev(part, step, s):
        if part ^ step == 0:
            return at_xy((gx + s) % ring, gy)
        return at_xy(gx, (gy + s) % ring)

    def pair_and_first(t, part, arrived):
        term, b = terms[t], bufs[t]
        arrived.wait_recv()
        lo, n = term.start[part], term.part[part]
        span = slice(lo, lo + n)
        b[2][span] = (b[0][core, span].astype(F32) + b[1][span].astype(F32)).astype(BF16)
        step = term.first[part]
        out = []
        for s in range(1, ring):
            peer = (ring_pos(part, 0) + s) % ring
            src = b[2].at[pl.ds(pl.multiple_of(lo + peer * step, 16), step)]
            out.append(send(src, b[3 + part].at[s - 1], ring_dev(part, 0, s)))
        return out

    def second(t, part, arrived):
        term, b = terms[t], bufs[t]
        for copy in arrived:
            copy.wait_recv()
        lo, n = term.start[part], term.first[part]
        mine = pl.ds(pl.multiple_of(lo + ring_pos(part, 0) * n, 16), n)
        total = b[2][mine].astype(F32)
        for s in range(ring - 1):
            total = total + b[3 + part][s].astype(F32)
        b[5 + part][...] = total.astype(BF16)
        step = term.second[part]
        out = []
        for s in range(1, ring):
            peer = (ring_pos(part, 1) + s) % ring
            src = b[5 + part].at[pl.ds(pl.multiple_of(peer * step, 16), step)]
            out.append(send(src, b[7 + part].at[s - 1], ring_dev(part, 1, s)))
        return out

    def third(t, arrived):
        term, b = terms[t], bufs[t]
        at = 0
        for part in (0, 1):
            for copy in arrived[part]:
                copy.wait_recv()
            n = term.second[part]
            mine = pl.ds(pl.multiple_of(ring_pos(part, 1) * n, 16), n)
            total = b[5 + part][mine].astype(F32)
            for s in range(ring - 1):
                total = total + b[7 + part][s].astype(F32)
            b[9][at : at + n] = total
            at += n
        if at < depth * term.zrows:
            b[9][at:] = jnp.zeros((depth * term.zrows - at, 128), F32)
        b[14][...] = b[9][...].reshape(depth, term.zrows, 128).astype(BF16)
        out = []
        for s in range(1, depth):
            peer = (lat + s) % depth
            out.append(send(b[14].at[peer], b[10].at[s - 1], (peer, lon)))
        return out

    def fourth(t, arrived):
        term, b = terms[t], bufs[t]
        for copy in arrived:
            copy.wait_recv()
        mine = pl.ds(pl.multiple_of(lat * term.zrows, 8), term.zrows)
        total = b[9][mine]
        for s in range(depth - 1):
            total = total + b[10][s].astype(F32)
        b[11][...] = total.astype(BF16)
        b[12][lat] = total.astype(BF16)
        return [
            send(b[11], b[12].at[lat], ((lat + s) % depth, lon)) for s in range(1, depth)
        ]

    def fifth(t, arrived):
        term, b = terms[t], bufs[t]
        for copy in arrived:
            copy.wait_recv()
        at, outs = 0, []
        whole = b[12][...].astype(F32).reshape(depth * term.zrows, 128)
        for part in (0, 1):
            n = term.second[part]
            place = term.start[part] + ring_pos(part, 0) * term.first[part] + ring_pos(part, 1) * n
            here = pl.ds(pl.multiple_of(place, 16), n)
            b[13][core, here] = whole[at : at + n].astype(BF16)
            at += n
            block = b[13].at[core, here]
            outs.append([send(block, block, ring_dev(part, 1, s)) for s in range(1, ring)])
        return outs

    def sixth(t, arrived):
        term, b = terms[t], bufs[t]
        outs = []
        for part in (0, 1):
            for copy in arrived[part]:
                copy.wait_recv()
            n = term.first[part]
            place = term.start[part] + ring_pos(part, 0) * n
            block = b[13].at[core, pl.ds(pl.multiple_of(place, 16), n)]
            outs.append([send(block, block, ring_dev(part, 0, s)) for s in range(1, ring)])
        return outs

    def seventh(t, arrived):
        b = bufs[t]
        for part in (0, 1):
            for copy in arrived[part]:
                copy.wait_recv()
        return send(b[13].at[core], b[13].at[core], sibling)

    stores = []

    def store(src, dst):
        copy = pltpu.make_async_copy(src, dst, store_sem.at[len(stores)])
        copy.start()
        stores.append(copy)

    for load in loads[:4]:
        load.wait()
    pre_one[...] = dot(x_v[...], wr_v[...]) * gr[...] + br[...]
    mid_one = smooth(pre_one[...]).astype(BF16)
    hi, wi = slice(1, 1 + h2n), slice(1, 1 + w2n)
    p_one[hi, wi] = dot(perm[...], mid_one).astype(BF16).reshape(h2n, w2n, 16, chan_mid)
    pl.semaphore_wait(barrier, len(greet))
    wait_one = halo(p_one)
    for load in loads[4:]:
        load.wait()
    lab_rows = batch * width
    pixel = lax.broadcasted_iota(jnp.int32, (pixels, lab_rows), 0)
    row = (pixel // (height * width)) * width + pixel % width
    row_hot = jnp.where(
        row == lax.broadcasted_iota(jnp.int32, (pixels, lab_rows), 1), 1.0, 0.0
    ).astype(BF16)
    picked = dot(row_hot, label_v[...].astype(F32).astype(BF16))
    pixel = lax.broadcasted_iota(jnp.int32, (pixels, height), 0)
    lane_hot = (pixel // width) % height == lax.broadcasted_iota(jnp.int32, (pixels, height), 1)
    label = jnp.sum(jnp.where(lane_hot, picked, 0.0), axis=1, keepdims=True)
    weight = class_weight[0, 0]
    for k in range(1, class_weight.shape[1]):
        weight = jnp.where(label > k - 0.5, class_weight[0, k], weight)
    pw[...] = jnp.broadcast_to(weight, pw.shape)
    total = dot(tap(p_one, 1, 1), wd_v[4])
    wait_one()
    for i in (0, 1, 2, 3, 5, 6, 7, 8):
        total = total + dot(tap(p_one, i // 3, i % 3), wd_v[i])
    pre_two = to_natural(total * gd[...] + bd[...])
    mid_two = smooth(pre_two).astype(BF16)
    slope_two[...] = slope(pre_two) * gd[...]

    blocks = chan_in // 256
    total = None
    for j in range(blocks):
        cols = slice(j * 256, (j + 1) * 256)
        w_block = we_v[:, cols]
        pre_three = dot(mid_two, w_block) * ge[:, cols] + be[:, cols] + x_v[:, cols].astype(F32)
        full = go_v[:, cols].astype(F32) * pw[...] * slope(pre_three)
        gfull[:, cols] = full
        grad_three = (full * ge[:, cols]).astype(BF16)
        gthree[:, cols] = grad_three
        term = dot_rt(grad_three, w_block)
        total = term if total is None else total + term
    grad_two = (total * slope_two[...]).astype(BF16)
    p_two[hi, wi] = dot(perm[...], grad_two).astype(BF16).reshape(h2n, w2n, 16, chan_mid)
    wait_two = halo(p_two)

    for j in range(blocks):
        put_term(0, j * 256, dot_lt(mid_two, gthree[:, j * 256 : (j + 1) * 256]))
    e_core = [core_send(0, 0), core_send(0, 1)]
    center = tap(p_two, 1, 1)
    taps_a = terms[1].ra // chan_mid
    d_core = []
    for i in range(9):
        put_term(1, i * chan_mid, dot_lt(tap(p_one, i // 3, i % 3), center))
        if i == taps_a - 1:
            d_core.append(core_send(1, 0))
            e_first = [pair_and_first(0, part, e_core[part]) for part in (0, 1)]
    d_core.append(core_send(1, 1))

    total = dot_rt(center, wd_v[4])
    d_first = [pair_and_first(1, 0, d_core[0])]
    wait_two()
    for i in (0, 1, 2, 3, 5, 6, 7, 8):
        total = total + dot_rt(tap(p_two, 2 - i // 3, 2 - i % 3), wd_v[i])
        if i == 3:
            d_first.append(pair_and_first(1, 1, d_core[1]))
    grad_one = (to_natural(total) * slope(pre_one[...]) * gr[...]).astype(BF16)
    r_core = []
    for j in range(2):
        half = chan_in // 2
        put_term(2, j * half, dot_lt(x_v[:, j * half : (j + 1) * half], grad_one))
        r_core.append(core_send(2, j))
    e_second = [second(0, part, e_first[part]) for part in (0, 1)]
    for j in range(blocks):
        cols = slice(j * 256, (j + 1) * 256)
        gi_v[:, cols] = (dot_rt(grad_one, wr_v[cols, :]) + gfull[:, cols]).astype(BF16)
    store(gi_v, gi_hbm)
    r_first = [pair_and_first(2, part, r_core[part]) for part in (0, 1)]
    e_third = third(0, e_second)
    d_second = [second(1, part, d_first[part]) for part in (0, 1)]
    r_second = [second(2, part, r_first[part]) for part in (0, 1)]
    d_third = third(1, d_second)
    e_fourth = fourth(0, e_third)
    r_third = third(2, r_second)
    d_fourth = fourth(1, d_third)
    e_fifth = fifth(0, e_fourth)
    r_fourth = fourth(2, r_third)
    d_fifth = fifth(1, d_fourth)
    e_sixth = sixth(0, e_fifth)
    r_fifth = fifth(2, r_fourth)
    d_sixth = sixth(1, d_fifth)
    e_last = seventh(0, e_sixth)
    r_sixth = sixth(2, r_fifth)
    d_last = seventh(1, d_sixth)
    r_last = seventh(2, r_sixth)

    e_last.wait_recv()
    for side in (0, 1):
        for j in range(blocks):
            first = j * 256 + side * 128
            store(
                bufs[0][13].at[side, j * 256 : (j + 1) * 256], gexp_hbm.at[:, first : first + 128]
            )
    d_last.wait_recv()
    for side in (0, 1):
        store(bufs[1][13].at[side], gdil_hbm.at[:, side * 128 : (side + 1) * 128])
    r_last.wait_recv()
    for side in (0, 1):
        store(bufs[2][13].at[side], gred_hbm.at[:, side * 128 : (side + 1) * 128])
    halo_copies = {id(copy) for _, copy, _ in guarded}
    for dl, copy, on in guarded:
        on(dl, False, copy.wait_send)
    for copy in copies:
        if id(copy) not in halo_copies:
            copy.wait_send()
    for copy in stores:
        copy.wait()


def per_device(
    ring,
    depth,
    inputs,
    w_reduce,
    gain_reduce,
    bias_reduce,
    w_dilated,
    gain_dilated,
    bias_dilated,
    w_expand,
    gain_expand,
    bias_expand,
    grad_out,
    labels,
    class_weight,
):
    batch, height, width, chan_in = inputs.shape
    chan_mid = w_reduce.shape[1]
    pixels = batch * height * width
    half = chan_in // 2
    terms = [
        Term(half, half, ring, depth),
        Term(5 * chan_mid, 4 * chan_mid, ring, depth),
        Term(half, half, ring, depth),
    ]
    scratch = [
        pltpu.VMEM((pixels, chan_in), BF16),
        pltpu.VMEM((chan_in, chan_mid), BF16),
        pltpu.VMEM((1, chan_mid), F32),
        pltpu.VMEM((1, chan_mid), F32),
        pltpu.VMEM((9, chan_mid, chan_mid), BF16),
        pltpu.VMEM((1, chan_mid), F32),
        pltpu.VMEM((1, chan_mid), F32),
        pltpu.VMEM((chan_mid, chan_in), BF16),
        pltpu.VMEM((1, chan_in), F32),
        pltpu.VMEM((1, chan_in), F32),
        pltpu.VMEM((pixels, chan_in), BF16),
        pltpu.VMEM((batch * width, height), jnp.int32),
        pltpu.VMEM((pixels, 1), F32),
        pltpu.VMEM((pixels, pixels), BF16),
        pltpu.VMEM((pixels, pixels), BF16),
        pltpu.VMEM((pixels, chan_mid), F32),
        pltpu.VMEM((pixels, chan_mid), F32),
        pltpu.VMEM((pixels, chan_in), F32),
        pltpu.VMEM((pixels, chan_in), BF16),
        pltpu.VMEM((height // 2 + 2, width // 2 + 2, 16, chan_mid), BF16),
        pltpu.VMEM((height // 2 + 2, width // 2 + 2, 16, chan_mid), BF16),
        pltpu.VMEM((pixels, chan_in), BF16),
    ]
    for term in terms:
        scratch += term.scratch(ring, depth)
    n_remote = 16 + 3 * (2 + 8 * (ring - 1) + 2 * (depth - 1) + 1)
    scratch += [
        pltpu.SemaphoreType.DMA((12,)),
        pltpu.SemaphoreType.DMA((2 * (chan_in // 256) + 5,)),
        pltpu.SemaphoreType.DMA((n_remote,)),
        pltpu.SemaphoreType.DMA((n_remote,)),
    ]
    anywhere = pl.BlockSpec(memory_space=pl.ANY)
    smem = pl.BlockSpec(memory_space=pltpu.SMEM)
    grad_inputs, grad_reduce, grad_dilated, grad_expand = pl.pallas_call(
        functools.partial(
            kernel, ring, depth, terms, (batch, height, width, chan_in, chan_mid)
        ),
        out_shape=(
            jax.ShapeDtypeStruct((pixels, chan_in), BF16),
            jax.ShapeDtypeStruct((chan_in, chan_mid), BF16),
            jax.ShapeDtypeStruct((9 * chan_mid, chan_mid), BF16),
            jax.ShapeDtypeStruct((chan_mid, chan_in), BF16),
        ),
        in_specs=[anywhere] * 12 + [smem],
        out_specs=(anywhere,) * 4,
        scratch_shapes=scratch,
        compiler_params=pltpu.CompilerParams(
            collective_id=0, has_side_effects=True, vmem_limit_bytes=60 * 2**20
        ),
    )(
        inputs.reshape(pixels, chan_in),
        w_reduce,
        gain_reduce.reshape(1, -1),
        bias_reduce.reshape(1, -1),
        w_dilated.reshape(9, chan_mid, chan_mid),
        gain_dilated.reshape(1, -1),
        bias_dilated.reshape(1, -1),
        w_expand,
        gain_expand.reshape(1, -1),
        bias_expand.reshape(1, -1),
        grad_out.reshape(pixels, chan_in),
        labels.transpose(0, 2, 1).reshape(batch * width, height),
        class_weight.reshape(1, -1),
    )
    return (
        grad_inputs.reshape(batch, height, width, chan_in),
        grad_reduce,
        grad_dilated.reshape(3, 3, chan_mid, chan_mid),
        grad_expand,
    )


def solution(mesh):
    ring = math.isqrt(mesh.shape["lon"] // 2)
    field = P(None, "lat", "lon", None)
    return jax.shard_map(
        functools.partial(per_device, ring, mesh.shape["lat"]),
        mesh=mesh,
        in_specs=(field,) + (P(),) * 9 + (field, P(None, "lat", "lon"), P()),
        out_specs=(field, P(), P(), P()),
        check_vma=False,
    )
```
